512 devices in a mesh: grp: 64 (over x, z, core), tp: 8 (over y).
Axes of the slice: x: 4, y: 8, z: 8, core: 2. Of those that a mesh axis runs over, the one named last changes fastest.
Arguments:
- patches: bfloat16 [65536, 1280], P(('grp', 'tp')), may hold values from -6 to 6
- pictures: int32 [64, 1024], P('grp', 'tp'), may hold values from 0 to 1, as said below
- vis_qkv: bfloat16 [3, 1280, 1280], P(None, 'tp'), as said below
- vis_out: bfloat16 [1280, 1280], P(None, 'grp'), may hold values from -0.15625 to 0.15625
- merge_w: bfloat16 [1280, 5120], P('tp'), may hold values from -0.078125 to 0.078125
- text: bfloat16 [65536, 1280], P(('grp', 'tp')), may hold values from -6 to 6
- places: int32 [16384], P(('grp', 'tp')), may hold values from 0 to 65535, as said below
- segments: int32 [64, 1024], P('grp', 'tp'), may hold values from 0 to 3, never falling along the last dimension, each value on 1 to 512 neighbouring positions
- txt_qkv: bfloat16 [3, 1280, 1280], P(None, 'tp'), as said below
- txt_out: bfloat16 [1280, 1280], P(None, 'grp'), may hold values from -0.15625 to 0.15625
Outputs:
- hidden_out: bfloat16 [65536, 1280], P(('grp', 'tp'))
The draws below stay inside these ranges and needn't reach their ends.
Inputs may be any that keep to these rules, and one draw needn't show every extreme that they name: `pictures`: within each row, picture numbers never fall; each picture is a run of whole aligned blocks of 4 positions and covers at least a quarter of the row, rounded down to whole blocks of 4 (at least one block). Row 0 holds one picture, row 1 two, the others one or two. `places`: all positions are distinct. The image rows of one device (aligned blocks of 32 rows, devices in the order of the placement) go to tokens held by the device of the same tp index in their token group: to 16 different token groups, exactly 2 rows to each. For each tp index, one token group receives 2 rows from every device of that tp index. `vis_qkv`: the query and key parts of a head may be correlated. `txt_qkv`: the query and key parts of a head may be correlated.
All inputs are finite; a program needn't handle non-finite values.
Results may differ from the reference program's by a relative error of at most 0.01.
Values may be sent and summed in bfloat16 or wider, within the bound.
A program may use at most 64 MiB of HBM per device.

```python
import math
import jax
import jax.numpy as jnp
import numpy as np
from jax import lax

D = 1280
HEADS = 16
HEAD_DIM = 80
TOK_DEV = 128
SEND_CAP = 2
MERGED_DEV = 32
GROUP_PATCHES = 1024
GROUP_TOKENS = 1024
PATCHES_ALL = 65536
MERGED_ALL = 16384
TOKENS = 65536
N_GRP = 64
N_TP = 8


def projection_weights(key):
    stacked = jax.random.normal(jax.random.fold_in(key, 11), (3, D, D), jnp.float32) * D ** (-0.5)
    return jnp.transpose(stacked, (0, 2, 1))


def draw_vis_qkv(key, part):
    return projection_weights(jax.random.fold_in(key, 101)).astype(jnp.bfloat16)


def draw_txt_qkv(key, part):
    return projection_weights(jax.random.fold_in(key, 202)).astype(jnp.bfloat16)


def draw_pictures(key, part):
    units = GROUP_PATCHES // 4
    least = max(1, units // 4)
    cut_at = jax.random.randint(jax.random.fold_in(key, 303), (N_GRP,), least, units + 1)
    group_ids = jnp.arange(N_GRP, dtype=jnp.int32)
    cut_at = jnp.where(group_ids == 0, units, cut_at)
    cut_at = jnp.where(group_ids == 1, units // 2, cut_at)
    cut_at = jnp.where(units - cut_at < least, units, cut_at)
    unit_ids = jnp.arange(units, dtype=jnp.int32)
    labels = (unit_ids[None, :] >= cut_at[:, None]).astype(jnp.int32)
    return jnp.repeat(labels, 4, axis=1)


def draw_places(key, part):
    pairs = MERGED_DEV // SEND_CAP
    base_key = jax.random.fold_in(key, 404)
    hot_group = jax.random.randint(jax.random.fold_in(base_key, 1), (N_TP,), 0, N_GRP)
    noise = jax.random.randint(jax.random.fold_in(base_key, 2), (N_TP, N_GRP, N_GRP), 0, 1 << 20)
    targets = jnp.arange(N_GRP, dtype=jnp.int32)
    scores = noise * N_GRP + targets[None, None, :]
    scores = jnp.where(targets[None, None, :] == hot_group[:, None, None], 1 << 28, scores)
    chosen = jnp.argsort(-scores, axis=-1)[:, :, :pairs].astype(jnp.int32)
    sends = jnp.sum((chosen[..., None] == targets[None, None, None, :]).astype(jnp.int32), axis=2)
    before = jnp.cumsum(sends, axis=1) - sends
    order_rank = jnp.take_along_axis(before, chosen, axis=2)
    within = SEND_CAP * order_rank[..., None] + jnp.arange(SEND_CAP, dtype=jnp.int32)
    tp_ids = jnp.arange(N_TP, dtype=jnp.int32)
    spots = chosen[..., None] * GROUP_TOKENS + tp_ids[:, None, None, None] * TOK_DEV + within
    return jnp.transpose(spots, (1, 0, 2, 3)).reshape(MERGED_ALL).astype(jnp.int32)


def levels(own_key, extent, cuts, low, top_value):
    def one(position, shards_of):
        heights = jax.random.uniform(jax.random.fold_in(jax.random.fold_in(own_key, 6), position), (shards_of,), jnp.float32, low / len(cuts), top_value / len(cuts))
        return jnp.repeat(jnp.exp(heights), extent[position] // shards_of).reshape((-1,) + (1,) * (len(extent) - position - 1))

    factor_of = one(*cuts[0])
    for cut in cuts[1:]:
        factor_of = factor_of * one(*cut)
    return factor_of


def split_up(number_of, total, limit, lean):
    portions = [(1 << 20) // math.isqrt(standing ** lean) + 1 for standing in range(2, number_of + 1)]
    spare, counts = total - limit - (number_of - 1), [1] * (number_of - 1)
    while spare > 0:
        candidates = [i for i in range(number_of - 1) if counts[i] < limit]
        pool, left = sum([portions[i] for i in candidates]), spare
        for i in candidates:
            extra = min(limit - counts[i], max(1, left * portions[i] // pool), spare)
            counts[i] = counts[i] + extra
            spare = spare - extra
    return np.array([limit] + counts)


def uneven(key, amount, total, limit, lean):
    if amount == 2:
        one = jax.random.randint(key, (), max(1, total - limit), min(limit, total - 1) + 1)
        return jnp.stack([one, total - one])
    lengths = jnp.asarray(split_up(amount, total, limit, lean), jnp.int32)
    pairs = (amount - 1) // 2
    giver, taker = lengths[1:1 + 2 * pairs:2], lengths[2:2 + 2 * pairs:2]
    room = jnp.minimum(giver - 1, limit - taker)
    passed = jax.random.randint(jax.random.fold_in(key, 1), (pairs,), 0, 1 << 20) % (room + 1)
    lengths = lengths.at[1:1 + 2 * pairs:2].set(giver - passed).at[2:2 + 2 * pairs:2].set(taker + passed)
    return lengths[jax.random.permutation(jax.random.fold_in(key, 2), amount)]


def normal_values(stream_key, shape, scale, limit, split=(), held_as=jnp.bfloat16):
    result = jax.random.normal(stream_key, shape, jnp.float32) * scale
    if len(split) > 0:
        result = levels(stream_key, shape, split, -0.22, 0.18) * result
    return jnp.clip(result, min=-limit, max=limit).astype(held_as)


def setup_inputs(seed: int = 0) -> dict:
    streams_of = jax.random.split(jax.random.key(seed), 11)
    return {
        "patches": normal_values(streams_of[0], (PATCHES_ALL, D), 1.0, 6.0, ((0, 512),)),
        "pictures": draw_pictures(jax.random.fold_in(streams_of[10], 71), 0),
        "vis_qkv": draw_vis_qkv(jax.random.fold_in(streams_of[10], 71), 0),
        "vis_out": normal_values(streams_of[3], (D, D), D ** -0.5, 0.15625, ((1, 64),)),
        "merge_w": normal_values(streams_of[4], (D, 4 * D), (4 * D) ** -0.5, 0.078125, ((0, 8),)),
        "text": normal_values(streams_of[5], (TOKENS, D), 1.0, 6.0, ((0, 512),)),
        "places": draw_places(jax.random.fold_in(streams_of[10], 71), 0),
        "segments": jax.vmap(lambda own: jnp.searchsorted(jnp.cumsum(uneven(own, 4, GROUP_TOKENS, GROUP_TOKENS // 2, 2)), jnp.arange(GROUP_TOKENS), side="right"))(jax.random.split(streams_of[7], N_GRP)).reshape((N_GRP, GROUP_TOKENS)).astype(jnp.int32),
        "txt_qkv": draw_txt_qkv(jax.random.fold_in(streams_of[10], 71), 0),
        "txt_out": normal_values(streams_of[9], (D, D), D ** -0.5, 0.15625, ((1, 64),)),
    }


EPSILON = 1e-05
MASKED = -1e+30

def layer_norm(rows):
    widened = rows.astype(jnp.float32)
    row_mean = lax.optimization_barrier(jnp.mean(widened, axis=-1, keepdims=True))
    centred = widened - row_mean
    spread = lax.optimization_barrier(jnp.mean(centred * centred, axis=-1, keepdims=True))
    return (centred * lax.rsqrt(spread + EPSILON)).astype(jnp.bfloat16)

def times_transpose(left, right):
    return lax.dot_general(left, right, (((1,), (1,)), ((), ())), preferred_element_type=jnp.float32)

def attend(queries, key_rows, value_rows, allowed):
    count = queries.shape[0]
    q_heads = queries.astype(jnp.float32).reshape(count, HEADS, HEAD_DIM)
    k_heads = key_rows.astype(jnp.float32).reshape(count, HEADS, HEAD_DIM)
    v_heads = value_rows.astype(jnp.float32).reshape(count, HEADS, HEAD_DIM)
    scores = jnp.einsum('qhd,khd->hqk', q_heads, k_heads) * HEAD_DIM ** (-0.5)
    scores = jnp.where(allowed[None], scores, MASKED)
    row_max = lax.optimization_barrier(jnp.max(scores, axis=-1, keepdims=True))
    weights = jnp.exp(scores - row_max)
    prob_bf = (weights / lax.optimization_barrier(jnp.sum(weights, axis=-1, keepdims=True))).astype(jnp.bfloat16)
    mixed = jnp.einsum('hqk,khd->qhd', prob_bf.astype(jnp.float32), v_heads)
    return mixed.astype(jnp.bfloat16).reshape(count, D)

def group_attention(normed, weights, labels, causal):
    queries = times_transpose(normed, weights[0]).astype(jnp.bfloat16)
    key_rows = times_transpose(normed, weights[1]).astype(jnp.bfloat16)
    value_rows = times_transpose(normed, weights[2]).astype(jnp.bfloat16)
    allowed = labels[:, None] == labels[None, :]
    if causal:
        order = jnp.arange(normed.shape[0], dtype=jnp.int32)
        allowed = allowed & (order[:, None] >= order[None, :])
    return attend(queries, key_rows, value_rows, allowed)

def reference(patches, pictures, vis_qkv, vis_out, merge_w, text, places, segments, txt_qkv, txt_out):
    patch_normed = layer_norm(patches).reshape(N_GRP, GROUP_PATCHES, D)
    vis_attn = lax.map(lambda group_item: group_attention(group_item[0], vis_qkv, group_item[1], False), (patch_normed, pictures))
    vis_attn = vis_attn.reshape(PATCHES_ALL, D)
    vis_hidden = (patches.astype(jnp.float32) + jnp.dot(vis_attn, vis_out, preferred_element_type=jnp.float32)).astype(jnp.bfloat16)
    merged = layer_norm(vis_hidden).reshape(MERGED_ALL, 4 * D)
    image_rows = times_transpose(merged, merge_w).astype(jnp.bfloat16)
    prompt = text.at[places].set(image_rows)
    token_normed = layer_norm(prompt).reshape(N_GRP, GROUP_TOKENS, D)
    txt_attn = lax.map(lambda group_item: group_attention(group_item[0], txt_qkv, group_item[1], True), (token_normed, segments))
    txt_attn = txt_attn.reshape(TOKENS, D)
    return (prompt.astype(jnp.float32) + jnp.dot(txt_attn, txt_out, preferred_element_type=jnp.float32)).astype(jnp.bfloat16)
```

```python
import functools

import jax
import jax.numpy as jnp
from jax import lax
from jax.experimental import pallas as pl
from jax.experimental.pallas import tpu as pltpu
from jax.sharding import PartitionSpec as P

HEAD_DIM = 80
SEND_CAP = 2
N_TP = 8
N_Z = 8
N_X = 4
SHARD = 20
SHARD_PAD = 24
LANES = 128


EPSILON = 1e-05
MASKED = -1e30
MESH = pl.DeviceIdType.MESH


def layer_norm(rows):
    widened = rows.astype(jnp.float32)
    row_mean = jnp.mean(widened, axis=-1, keepdims=True)
    centred = widened - row_mean
    spread = jnp.mean(centred * centred, axis=-1, keepdims=True)
    return (centred * lax.rsqrt(spread + EPSILON)).astype(jnp.bfloat16)


def times_transpose(left, right):
    return lax.dot_general(
        left, right, (((1,), (1,)), ((), ())), preferred_element_type=jnp.float32
    )


def wrap(value, count):
    return lax.rem(value + count, count)


def greet(devices):
    barrier = pltpu.get_barrier_semaphore()
    for device in devices:
        pl.semaphore_signal(barrier, inc=1, device_id=device, device_id_type=MESH)
    pl.semaphore_wait(barrier, len(devices))


def gather_kernel(with_extras, *refs):
    if with_extras:
        own, own_label, own_shard, rows, labels, shards, *sems = refs
        row_send, row_recv, local_sem, lab_send, lab_recv, z_send, z_recv, x_send, x_recv = sems
    else:
        own, rows, row_send, row_recv, local_sem = refs
    tp = lax.axis_index("tp")
    grp = lax.axis_index("grp")
    core = lax.rem(grp, 2)
    z_here = lax.rem(grp // 2, N_Z)
    x_here = grp // (2 * N_Z)
    half = own.shape[0] // 2

    def at_xz(x, z):
        return {"grp": (x * N_Z + z) * 2 + core}

    def remote(src, dst, send, recv, device):
        return pltpu.make_async_remote_copy(
            src_ref=src,
            dst_ref=dst,
            send_sem=send,
            recv_sem=recv,
            device_id=device,
            device_id_type=MESH,
        )

    neighbours = [{"tp": wrap(tp + 1, N_TP)}, {"tp": wrap(tp - 1, N_TP)}]
    if with_extras:
        z_next = [at_xz(x_here, wrap(z_here + 1, N_Z)), at_xz(x_here, wrap(z_here - 1, N_Z))]
        x_peers = [at_xz(wrap(x_here + d, N_X), z_here) for d in range(1, N_X)]
        greet(neighbours + z_next + x_peers)
    else:
        greet(neighbours)

    def row_copy(way, step, part):
        block = wrap(tp - step, N_TP) if way == 0 else wrap(tp + step, N_TP)
        span = pl.ds(part * half, half)
        dst = rows.at[block, span]
        src = own.at[span] if step == 0 else dst
        slot = (way * 4 + step) * 2 + part
        return remote(src, dst, row_send.at[slot], row_recv.at[slot], neighbours[way])

    def label_copy(way, step):
        block = wrap(tp - step, N_TP) if way == 0 else wrap(tp + step, N_TP)
        dst = labels.at[block]
        src = own_label if step == 0 else dst
        slot = way * 4 + step
        return remote(src, dst, lab_send.at[slot], lab_recv.at[slot], neighbours[way])

    def shard_copy(way, step, part):
        block = wrap(z_here - step, N_Z) if way == 0 else wrap(z_here + step, N_Z)
        piece = shards.at[block, pl.ds(part * 2, 2)]
        slot = (way * 4 + step) * 2 + part
        return remote(piece, piece, z_send.at[slot], z_recv.at[slot], z_next[way])

    local = [pltpu.make_async_copy(own, rows.at[tp], local_sem.at[0])]
    if with_extras:
        local.append(pltpu.make_async_copy(own_label, labels.at[tp], local_sem.at[1]))
        own_place = shards.at[z_here, x_here]
        local.append(pltpu.make_async_copy(own_shard, own_place, local_sem.at[2]))
    for copy in local:
        copy.start()
    pending = []

    def start(copy):
        copy.start()
        pending.append(copy)

    if with_extras:
        x_copies = [
            remote(own_shard, own_place, x_send.at[d], x_recv.at[d], x_peers[d])
            for d in range(N_X - 1)
        ]
        for copy in x_copies:
            start(copy)
    row_ring = {}
    for part in range(2):
        for way in range(2):
            row_ring[way, 0, part] = row_copy(way, 0, part)
            start(row_ring[way, 0, part])
    if with_extras:
        label_ring = {(way, 0): label_copy(way, 0) for way in range(2)}
        for way in range(2):
            start(label_ring[way, 0])
    for copy in local:
        copy.wait()
    if with_extras:
        for copy in x_copies:
            copy.wait_recv()
        shard_ring = {}
        for part in range(2):
            for way in range(2):
                shard_ring[way, 0, part] = shard_copy(way, 0, part)
                start(shard_ring[way, 0, part])
    for step in range(1, 4):
        for part in range(2):
            for way in range(2):
                row_ring[way, step - 1, part].wait_recv()
                if step < 3 or part == way:
                    row_ring[way, step, part] = row_copy(way, step, part)
                    start(row_ring[way, step, part])
            if with_extras:
                for way in range(2):
                    shard_ring[way, step - 1, part].wait_recv()
                    if step < 3 or part == way:
                        shard_ring[way, step, part] = shard_copy(way, step, part)
                        start(shard_ring[way, step, part])
        if with_extras:
            for way in range(2):
                label_ring[way, step - 1].wait_recv()
                if step < 3 or way == 0:
                    label_ring[way, step] = label_copy(way, step)
                    start(label_ring[way, step])
    for way in range(2):
        row_ring[way, 3, way].wait_recv()
        if with_extras:
            shard_ring[way, 3, way].wait_recv()
    if with_extras:
        label_ring[0, 3].wait_recv()
    for copy in pending:
        copy.wait_send()


def gather_rows(own, collective_id, own_label=None, own_shard=None):
    with_extras = own_label is not None
    vmem = pl.BlockSpec(memory_space=pltpu.VMEM)
    hbm = pl.BlockSpec(memory_space=pl.ANY)
    operands = [own]
    shapes = [jax.ShapeDtypeStruct((N_TP, *own.shape), own.dtype)]
    dma = pltpu.SemaphoreType.DMA
    scratch = [dma((16,)), dma((16,)), dma((3,))]
    if with_extras:
        operands += [own_label, own_shard]
        shapes.append(jax.ShapeDtypeStruct((N_TP, *own_label.shape), own_label.dtype))
        shapes.append(jax.ShapeDtypeStruct((N_Z, N_X, *own_shard.shape), own_shard.dtype))
        scratch += [dma((8,)), dma((8,)), dma((16,)), dma((16,)), dma((3,)), dma((3,))]
    return pl.pallas_call(
        functools.partial(gather_kernel, with_extras),
        out_shape=shapes,
        in_specs=[vmem] * len(operands),
        out_specs=[hbm] * len(shapes),
        scratch_shapes=scratch,
        compiler_params=pltpu.CompilerParams(collective_id=collective_id, has_side_effects=True),
    )(*operands)


PIECES = 4


def swap_kernel(with_shards, *refs):
    if with_shards:
        blocks, shards, received, other, send, recv, local_sem, core_send, core_recv = refs
    else:
        blocks, received, send, recv, local_sem = refs
    tp = lax.axis_index("tp")
    grp = lax.axis_index("grp")
    partner = {"grp": grp + 1 - 2 * lax.rem(grp, 2)}
    peers = [{"tp": wrap(tp + d, N_TP)} for d in range(1, N_TP)]
    greet(peers + [partner] if with_shards else peers)
    own = pltpu.make_async_copy(blocks.at[tp], received.at[tp], local_sem)
    own.start()
    copies = []
    for d in (4, 3, 5, 2, 6, 1, 7):
        copies.append(
            pltpu.make_async_remote_copy(
                src_ref=blocks.at[wrap(tp + d, N_TP)],
                dst_ref=received.at[tp],
                send_sem=send.at[d],
                recv_sem=recv.at[d],
                device_id=peers[d - 1],
                device_id_type=MESH,
            )
        )
    if with_shards:
        count = shards.shape[0] // PIECES
        for piece in range(PIECES):
            span = pl.ds(piece * count, count)
            copies.append(
                pltpu.make_async_remote_copy(
                    src_ref=shards.at[span],
                    dst_ref=other.at[span],
                    send_sem=core_send.at[piece],
                    recv_sem=core_recv.at[piece],
                    device_id=partner,
                    device_id_type=MESH,
                )
            )
    for copy in copies:
        copy.start()
    own.wait()
    for copy in copies:
        copy.wait()


def swap_blocks(blocks, collective_id, shards=None):
    with_shards = shards is not None
    vmem = pl.BlockSpec(memory_space=pltpu.VMEM)
    hbm = pl.BlockSpec(memory_space=pl.ANY)
    dma = pltpu.SemaphoreType.DMA
    scratch = [dma((N_TP,)), dma((N_TP,)), dma]
    operands, specs = [blocks], [vmem]
    if with_shards:
        operands.append(shards)
        specs.append(hbm)
        scratch += [dma((PIECES,)), dma((PIECES,))]
    return pl.pallas_call(
        functools.partial(swap_kernel, with_shards),
        out_shape=[jax.ShapeDtypeStruct(a.shape, a.dtype) for a in operands],
        in_specs=specs,
        out_specs=[hbm] * len(operands),
        scratch_shapes=scratch,
        compiler_params=pltpu.CompilerParams(collective_id=collective_id, has_side_effects=True),
    )(*operands)


def local_attention(queries, key_rows, value_rows, labels, causal):
    row_count, col_count = queries.shape
    heads_here = col_count // HEAD_DIM
    q_heads = queries.reshape(row_count, heads_here, HEAD_DIM)
    k_heads = key_rows.reshape(row_count, heads_here, HEAD_DIM)
    v_heads = value_rows.reshape(row_count, heads_here, HEAD_DIM)
    blocks = max(1, min(8, row_count // 512))
    block_rows = row_count // blocks
    inv_root = HEAD_DIM ** (-0.5)
    outputs = []
    for block_index in range(blocks):
        begin_row = block_index * block_rows
        end_key = begin_row + block_rows if causal else row_count
        scores = (
            jnp.einsum(
                "qhd,khd->hqk",
                q_heads[begin_row : begin_row + block_rows],
                k_heads[:end_key],
                preferred_element_type=jnp.float32,
            )
            * inv_root
        )
        allowed = labels[begin_row : begin_row + block_rows, None] == labels[None, :end_key]
        if causal:
            query_ids = jnp.arange(begin_row, begin_row + block_rows, dtype=jnp.int32)
            key_ids = jnp.arange(end_key, dtype=jnp.int32)
            allowed = allowed & (query_ids[:, None] >= key_ids[None, :])
        scores = jnp.where(allowed[None], scores, MASKED)
        row_max = jnp.max(scores, axis=-1, keepdims=True)
        weights = jnp.exp(scores - row_max)
        prob_bf = (weights / jnp.sum(weights, axis=-1, keepdims=True)).astype(jnp.bfloat16)
        mixed = jnp.einsum(
            "hqk,khd->qhd", prob_bf, v_heads[:end_key], preferred_element_type=jnp.float32
        )
        outputs.append(mixed.astype(jnp.bfloat16).reshape(block_rows, col_count))
    return jnp.concatenate(outputs, axis=0)


def attention_heads(gathered, weights, labels, causal):
    queries = times_transpose(gathered, weights[0]).astype(jnp.bfloat16)
    key_rows = times_transpose(gathered, weights[1]).astype(jnp.bfloat16)
    value_rows = times_transpose(gathered, weights[2]).astype(jnp.bfloat16)
    return local_attention(queries, key_rows, value_rows, labels, causal)


def attention_layer(rows, labels, qkv, columns, causal, first_id):
    shard = jnp.pad(columns.T, ((0, SHARD_PAD - SHARD), (0, 0)))
    gathered, all_labels, shards = gather_rows(layer_norm(rows), first_id, labels, shard)
    row_total = N_TP * rows.shape[0]
    heads = attention_heads(
        gathered.reshape(row_total, rows.shape[1]), qkv, all_labels.reshape(row_total), causal
    )
    blocks = heads.reshape(N_TP, rows.shape[0], heads.shape[1]).transpose(0, 2, 1)
    own_heads, other = swap_blocks(blocks, first_id + 1, shards)
    own_heads = own_heads.reshape(rows.shape[1], rows.shape[0])

    def project(part):
        flat = part.reshape(N_Z * N_X * SHARD_PAD, rows.shape[1])
        return jnp.dot(flat, own_heads, preferred_element_type=jnp.float32)

    here, there = project(shards), project(other)
    first = lax.rem(lax.axis_index("grp"), 2) == 0
    both = jnp.stack([jnp.where(first, here, there), jnp.where(first, there, here)])
    both = both.reshape(2, N_Z, N_X, SHARD_PAD, rows.shape[0])[:, :, :, :SHARD]
    projected = both.transpose(4, 2, 1, 0, 3).reshape(rows.shape)
    return (rows.astype(jnp.float32) + projected).astype(jnp.bfloat16)


def per_device(
    patches, pictures, vis_qkv, vis_out, merge_w, text, places, segments, txt_qkv, txt_out
):
    tp_count = lax.axis_size("tp")
    grp_count = lax.axis_size("grp")
    width = patches.shape[1]
    vis_hidden = attention_layer(patches, pictures, vis_qkv, vis_out, False, 0)
    merged = layer_norm(vis_hidden).reshape(patches.shape[0] // 4, 4 * width)
    (all_merged,) = gather_rows(merged, 2)
    row_total = places.shape[0]
    image_cols = times_transpose(
        all_merged.reshape(tp_count * row_total, 4 * width), merge_w
    ).astype(jnp.bfloat16)
    (image_parts,) = swap_blocks(image_cols.reshape(tp_count, row_total, -1), 3)
    image_rows = image_parts.transpose(1, 0, 2).reshape(row_total, width)
    tok_count = text.shape[0]
    group_tokens = tok_count * tp_count
    dest_group = places // group_tokens
    dest_local = places % tok_count
    row_ids = jnp.arange(row_total, dtype=jnp.int32)
    earlier = row_ids[:, None] > row_ids[None, :]
    same_dest = dest_group[:, None] == dest_group[None, :]
    slot_rank = jnp.sum((earlier & same_dest).astype(jnp.int32), axis=1)
    slot_index = dest_group * SEND_CAP + slot_rank
    slot_ids = jnp.arange(grp_count * SEND_CAP, dtype=jnp.int32)
    slot_pick = (slot_ids[:, None] == slot_index[None, :]).astype(jnp.bfloat16)
    marks = jnp.broadcast_to((dest_local + 1)[:, None], (row_total, LANES)).astype(jnp.bfloat16)
    send_rows = jnp.dot(
        slot_pick,
        jnp.concatenate([image_rows, marks], axis=1),
        preferred_element_type=jnp.float32,
    ).astype(jnp.bfloat16)
    send_rows = send_rows.reshape(grp_count, SEND_CAP, width + LANES)
    recv = lax.all_to_all(send_rows, "grp", split_axis=0, concat_axis=0, tiled=True)
    recv = recv.reshape(grp_count * SEND_CAP, width + LANES)
    recv_rows = recv[:, :width]
    recv_pos = recv[:, width].astype(jnp.int32) - 1
    position_hit = jnp.arange(tok_count, dtype=jnp.int32)[:, None] == recv_pos[None, :]
    placed = jnp.dot(
        position_hit.astype(jnp.bfloat16), recv_rows, preferred_element_type=jnp.float32
    ).astype(jnp.bfloat16)
    covered = jnp.any(position_hit, axis=1)
    prompt = jnp.where(covered[:, None], placed, text)
    return attention_layer(prompt, segments, txt_qkv, txt_out, True, 4)


def solution(mesh):
    placed = (
        P(("grp", "tp"), None),
        P("grp", "tp"),
        P(None, "tp", None),
        P(None, "grp"),
        P("tp", None),
        P(("grp", "tp"), None),
        P(("grp", "tp")),
        P("grp", "tp"),
        P(None, "tp", None),
        P(None, "grp"),
    )
    return jax.shard_map(
        per_device, mesh=mesh, in_specs=placed, out_specs=P(("grp", "tp"), None), check_vma=False
    )
```

```python
import functools

import jax
import jax.numpy as jnp
from jax import lax
from jax.experimental import pallas as pl
from jax.experimental.pallas import tpu as pltpu
from jax.sharding import PartitionSpec as P

HEAD_DIM = 80
SEND_CAP = 2
N_TP = 8
N_Z = 8
N_X = 4
SHARD = 20
SHARD_PAD = 24
LANES = 128


EPSILON = 1e-05
MASKED = -1e30
MESH = pl.DeviceIdType.MESH


def layer_norm(rows):
    widened = rows.astype(jnp.float32)
    row_mean = jnp.mean(widened, axis=-1, keepdims=True)
    centred = widened - row_mean
    spread = jnp.mean(centred * centred, axis=-1, keepdims=True)
    return (centred * lax.rsqrt(spread + EPSILON)).astype(jnp.bfloat16)


def times_transpose(left, right):
    return lax.dot_general(
        left, right, (((1,), (1,)), ((), ())), preferred_element_type=jnp.float32
    )


def wrap(value, count):
    return lax.rem(value + count, count)


def greet(devices):
    barrier = pltpu.get_barrier_semaphore()
    for device in devices:
        pl.semaphore_signal(barrier, inc=1, device_id=device, device_id_type=MESH)
    pl.semaphore_wait(barrier, len(devices))


def gather_kernel(with_extras, *refs):
    if with_extras:
        own, own_label, own_shard, rows, labels, shards, *sems = refs
        row_send, row_recv, local_sem, lab_send, lab_recv, z_send, z_recv, x_send, x_recv = sems
    else:
        own, rows, row_send, row_recv, local_sem = refs
    tp = lax.axis_index("tp")
    grp = lax.axis_index("grp")
    core = lax.rem(grp, 2)
    z_here = lax.rem(grp // 2, N_Z)
    x_here = grp // (2 * N_Z)
    half = own.shape[0] // 2

    def at_xz(x, z):
        return {"grp": (x * N_Z + z) * 2 + core}

    def remote(src, dst, send, recv, device):
        return pltpu.make_async_remote_copy(
            src_ref=src,
            dst_ref=dst,
            send_sem=send,
            recv_sem=recv,
            device_id=device,
            device_id_type=MESH,
        )

    neighbours = [{"tp": wrap(tp + 1, N_TP)}, {"tp": wrap(tp - 1, N_TP)}]
    if with_extras:
        z_next = [at_xz(x_here, wrap(z_here + 1, N_Z)), at_xz(x_here, wrap(z_here - 1, N_Z))]
        x_peers = [at_xz(wrap(x_here + d, N_X), z_here) for d in range(1, N_X)]
        greet(neighbours + z_next + x_peers)
    else:
        greet(neighbours)

    def row_copy(way, step, part):
        block = wrap(tp - step, N_TP) if way == 0 else wrap(tp + step, N_TP)
        span = pl.ds(part * half, half)
        dst = rows.at[block, span]
        src = own.at[span] if step == 0 else dst
        slot = (way * 4 + step) * 2 + part
        return remote(src, dst, row_send.at[slot], row_recv.at[slot], neighbours[way])

    def label_copy(way, step):
        block = wrap(tp - step, N_TP) if way == 0 else wrap(tp + step, N_TP)
        dst = labels.at[block]
        src = own_label if step == 0 else dst
        slot = way * 4 + step
        return remote(src, dst, lab_send.at[slot], lab_recv.at[slot], neighbours[way])

    def shard_copy(way, step, part):
        block = wrap(z_here - step, N_Z) if way == 0 else wrap(z_here + step, N_Z)
        piece = shards.at[block, pl.ds(part * 2, 2)]
        slot = (way * 4 + step) * 2 + part
        return remote(piece, piece, z_send.at[slot], z_recv.at[slot], z_next[way])

    local = [pltpu.make_async_copy(own, rows.at[tp], local_sem.at[0])]
    if with_extras:
        local.append(pltpu.make_async_copy(own_label, labels.at[tp], local_sem.at[1]))
        own_place = shards.at[z_here, x_here]
        local.append(pltpu.make_async_copy(own_shard, own_place, local_sem.at[2]))
    for copy in local:
        copy.start()
    pending = []

    def start(copy):
        copy.start()
        pending.append(copy)

    if with_extras:
        x_copies = [
            remote(own_shard, own_place, x_send.at[d], x_recv.at[d], x_peers[d])
            for d in range(N_X - 1)
        ]
        for copy in x_copies:
            start(copy)
    row_ring = {}
    for part in range(2):
        for way in range(2):
            row_ring[way, 0, part] = row_copy(way, 0, part)
            start(row_ring[way, 0, part])
    if with_extras:
        label_ring = {(way, 0): label_copy(way, 0) for way in range(2)}
        for way in range(2):
            start(label_ring[way, 0])
    for copy in local:
        copy.wait()
    if with_extras:
        for copy in x_copies:
            copy.wait_recv()
        shard_ring = {}
        for part in range(2):
            for way in range(2):
                shard_ring[way, 0, part] = shard_copy(way, 0, part)
                start(shard_ring[way, 0, part])
    for step in range(1, 4):
        for part in range(2):
            for way in range(2):
                row_ring[way, step - 1, part].wait_recv()
                if step < 3 or part == way:
                    row_ring[way, step, part] = row_copy(way, step, part)
                    start(row_ring[way, step, part])
            if with_extras:
                for way in range(2):
                    shard_ring[way, step - 1, part].wait_recv()
                    if step < 3 or part == way:
                        shard_ring[way, step, part] = shard_copy(way, step, part)
                        start(shard_ring[way, step, part])
        if with_extras:
            for way in range(2):
                label_ring[way, step - 1].wait_recv()
                if step < 3 or way == 0:
                    label_ring[way, step] = label_copy(way, step)
                    start(label_ring[way, step])
    for way in range(2):
        row_ring[way, 3, way].wait_recv()
        if with_extras:
            shard_ring[way, 3, way].wait_recv()
    if with_extras:
        label_ring[0, 3].wait_recv()
    for copy in pending:
        copy.wait_send()


def gather_rows(own, collective_id, own_label=None, own_shard=None):
    with_extras = own_label is not None
    vmem = pl.BlockSpec(memory_space=pltpu.VMEM)
    hbm = pl.BlockSpec(memory_space=pl.ANY)
    operands = [own]
    shapes = [jax.ShapeDtypeStruct((N_TP, *own.shape), own.dtype)]
    dma = pltpu.SemaphoreType.DMA
    scratch = [dma((16,)), dma((16,)), dma((3,))]
    if with_extras:
        operands += [own_label, own_shard]
        shapes.append(jax.ShapeDtypeStruct((N_TP, *own_label.shape), own_label.dtype))
        shapes.append(jax.ShapeDtypeStruct((N_Z, N_X, *own_shard.shape), own_shard.dtype))
        scratch += [dma((8,)), dma((8,)), dma((16,)), dma((16,)), dma((3,)), dma((3,))]
    return pl.pallas_call(
        functools.partial(gather_kernel, with_extras),
        out_shape=shapes,
        in_specs=[vmem] * len(operands),
        out_specs=[hbm] * len(shapes),
        scratch_shapes=scratch,
        compiler_params=pltpu.CompilerParams(collective_id=collective_id, has_side_effects=True),
    )(*operands)


PIECES = 4


def swap_kernel(with_shards, *refs):
    if with_shards:
        blocks, shards, received, other, send, recv, local_sem, core_send, core_recv = refs
    else:
        blocks, received, send, recv, local_sem = refs
    tp = lax.axis_index("tp")
    grp = lax.axis_index("grp")
    partner = {"grp": grp + 1 - 2 * lax.rem(grp, 2)}
    peers = [{"tp": wrap(tp + d, N_TP)} for d in range(1, N_TP)]
    greet(peers + [partner] if with_shards else peers)
    own = pltpu.make_async_copy(blocks.at[tp], received.at[tp], local_sem)
    own.start()
    copies = []
    for d in (4, 3, 5, 2, 6, 1, 7):
        copies.append(
            pltpu.make_async_remote_copy(
                src_ref=blocks.at[wrap(tp + d, N_TP)],
                dst_ref=received.at[tp],
                send_sem=send.at[d],
                recv_sem=recv.at[d],
                device_id=peers[d - 1],
                device_id_type=MESH,
            )
        )
    if with_shards:
        count = shards.shape[0] // PIECES
        for piece in range(PIECES):
            span = pl.ds(piece * count, count)
            copies.append(
                pltpu.make_async_remote_copy(
                    src_ref=shards.at[span],
                    dst_ref=other.at[span],
                    send_sem=core_send.at[piece],
                    recv_sem=core_recv.at[piece],
                    device_id=partner,
                    device_id_type=MESH,
                )
            )
    for copy in copies:
        copy.start()
    own.wait()
    for copy in copies:
        copy.wait()


def swap_blocks(blocks, collective_id, shards=None):
    with_shards = shards is not None
    vmem = pl.BlockSpec(memory_space=pltpu.VMEM)
    hbm = pl.BlockSpec(memory_space=pl.ANY)
    dma = pltpu.SemaphoreType.DMA
    scratch = [dma((N_TP,)), dma((N_TP,)), dma]
    operands, specs = [blocks], [vmem]
    if with_shards:
        operands.append(shards)
        specs.append(hbm)
        scratch += [dma((PIECES,)), dma((PIECES,))]
    return pl.pallas_call(
        functools.partial(swap_kernel, with_shards),
        out_shape=[jax.ShapeDtypeStruct(a.shape, a.dtype) for a in operands],
        in_specs=specs,
        out_specs=[hbm] * len(operands),
        scratch_shapes=scratch,
        compiler_params=pltpu.CompilerParams(collective_id=collective_id, has_side_effects=True),
    )(*operands)


Q_BLOCK = 256


def project_all(rows, weights):
    return lax.dot_general(
        weights, rows, (((1,), (1,)), ((), ())), preferred_element_type=jnp.float32
    )


def attend(projected, labels, store, causal):
    heads_here = projected.shape[0] // 3 // HEAD_DIM
    row_count = projected.shape[1]
    factor = HEAD_DIM ** (-0.5) * 1.4426950408889634
    key_labels = jnp.concatenate(
        [jnp.broadcast_to(label, (LANES, LANES)).T for label in labels], axis=0
    )
    keys = []
    for head in range(heads_here):
        begin = (heads_here + head) * HEAD_DIM
        keys.append(projected[begin : begin + HEAD_DIM].T.astype(jnp.bfloat16))
    lanes_per = Q_BLOCK // LANES
    for block in range(row_count // Q_BLOCK):
        first = block * Q_BLOCK
        end_key = first + Q_BLOCK if causal else row_count
        allowed = jnp.concatenate(
            [
                key_labels[:end_key] == labels[block * lanes_per + piece]
                for piece in range(lanes_per)
            ],
            axis=1,
        )
        if causal:
            key_ids = lax.broadcasted_iota(jnp.int32, (end_key, Q_BLOCK), 0)
            query_ids = lax.broadcasted_iota(jnp.int32, (end_key, Q_BLOCK), 1) + first
            allowed = allowed & (query_ids >= key_ids)
        for head in range(heads_here):
            begin = head * HEAD_DIM
            queries = projected[begin : begin + HEAD_DIM, first : first + Q_BLOCK]
            value_begin = (2 * heads_here + head) * HEAD_DIM
            values = projected[value_begin : value_begin + HEAD_DIM, :end_key]
            scores = jnp.dot(
                keys[head][:end_key],
                queries.astype(jnp.bfloat16),
                preferred_element_type=jnp.float32,
            )
            scores = jnp.where(allowed, scores, MASKED)
            top = jnp.max(scores, axis=0, keepdims=True)
            weights = jnp.exp2((scores - top) * factor)
            total = jnp.sum(weights, axis=0, keepdims=True)
            mixed = jnp.dot(
                values.astype(jnp.bfloat16),
                weights.astype(jnp.bfloat16),
                preferred_element_type=jnp.float32,
            )
            store(block, head, (mixed / total).astype(jnp.bfloat16))


def attention_kernel(causal, rows, weights, labels, out, projected):
    projected[...] = project_all(rows[...], weights[...])
    label_rows = [labels[part].astype(jnp.float32) for part in range(N_TP)]

    def store(block, head, mixed):
        for piece in range(Q_BLOCK // LANES):
            target = block * (Q_BLOCK // LANES) + piece
            out[target, head * HEAD_DIM : (head + 1) * HEAD_DIM, :] = mixed[
                :, piece * LANES : (piece + 1) * LANES
            ]

    attend(projected, label_rows, store, causal)


def attention_heads(gathered, weights, labels, causal):
    features = weights.shape[0] * weights.shape[1]
    vmem = pl.BlockSpec(memory_space=pltpu.VMEM)
    return pl.pallas_call(
        functools.partial(attention_kernel, causal),
        out_shape=jax.ShapeDtypeStruct((N_TP, weights.shape[1], LANES), jnp.bfloat16),
        in_specs=[vmem] * 3,
        out_specs=vmem,
        scratch_shapes=[pltpu.VMEM((features, gathered.shape[0]), jnp.float32)],
    )(gathered, weights.reshape(features, weights.shape[2]), labels)


def merge_kernel(own, weights_hbm, image, slots, weights, results, *sems):
    row_send, row_recv, col_send, col_recv, local_sem = sems
    tp = lax.axis_index("tp")
    half = own.shape[0] // 2
    greet([{"tp": wrap(tp + d, N_TP)} for d in range(1, N_TP)])
    neighbours = [{"tp": wrap(tp + 1, N_TP)}, {"tp": wrap(tp - 1, N_TP)}]

    def block_of(way, step):
        return wrap(tp - step, N_TP) if way == 0 else wrap(tp + step, N_TP)

    def row_copy(way, step, part):
        span = pl.ds(part * half, half)
        dst = slots.at[block_of(way, step), span]
        slot = (way * 4 + step) * 2 + part
        return pltpu.make_async_remote_copy(
            src_ref=own.at[span] if step == 0 else dst,
            dst_ref=dst,
            send_sem=row_send.at[slot],
            recv_sem=row_recv.at[slot],
            device_id=neighbours[way],
            device_id_type=MESH,
        )

    pending = []
    ring = {}

    def start(way, step, part):
        ring[way, step, part] = row_copy(way, step, part)
        ring[way, step, part].start()
        pending.append(ring[way, step, part])

    for part in range(2):
        for way in range(2):
            start(way, 0, part)
    fetch = pltpu.make_async_copy(weights_hbm, weights, local_sem.at[0])
    fetch.start()
    fetch.wait()

    def columns(block):
        return times_transpose(block, weights[...]).astype(jnp.bfloat16)

    results[tp] = columns(own[...])
    keep = pltpu.make_async_copy(results.at[tp], image.at[tp], local_sem.at[1])
    keep.start()
    arrivals = []

    def give(way, step):
        block = block_of(way, step)
        results[block] = columns(slots[block])
        copy = pltpu.make_async_remote_copy(
            src_ref=results.at[block],
            dst_ref=image.at[tp],
            send_sem=col_send.at[way * 5 + step],
            recv_sem=col_recv.at[way * 5 + step],
            device_id={"tp": block},
            device_id_type=MESH,
        )
        copy.start()
        pending.append(copy)
        arrivals.append(copy)

    for step in range(1, 4):
        for part in range(2):
            for way in range(2):
                ring[way, step - 1, part].wait_recv()
                if step < 3 or part == way:
                    start(way, step, part)
        for way in range(2):
            give(way, step)
    for way in range(2):
        ring[way, 3, way].wait_recv()
    give(0, 4)
    keep.wait()
    for copy in arrivals:
        copy.wait_recv()
    for copy in pending:
        copy.wait_send()


def merge_rows(merged, merge_w, collective_id):
    row_total, depth = merged.shape
    features = merge_w.shape[0]
    hbm = pl.BlockSpec(memory_space=pl.ANY)
    dma = pltpu.SemaphoreType.DMA
    return pl.pallas_call(
        merge_kernel,
        out_shape=jax.ShapeDtypeStruct((N_TP, row_total, features), jnp.bfloat16),
        in_specs=[pl.BlockSpec(memory_space=pltpu.VMEM), hbm],
        out_specs=hbm,
        scratch_shapes=[
            pltpu.VMEM((N_TP, row_total, depth), jnp.bfloat16),
            pltpu.VMEM((features, depth), jnp.bfloat16),
            pltpu.VMEM((N_TP, row_total, features), jnp.bfloat16),
            dma((16,)),
            dma((16,)),
            dma((10,)),
            dma((10,)),
            dma((2,)),
        ],
        compiler_params=pltpu.CompilerParams(collective_id=collective_id, has_side_effects=True),
    )(merged, merge_w)


def attention_layer(rows, labels, qkv, columns, causal, first_id):
    shard = jnp.pad(columns.T, ((0, SHARD_PAD - SHARD), (0, 0)))
    gathered, all_labels, shards = gather_rows(layer_norm(rows), first_id, labels, shard)
    row_total = N_TP * rows.shape[0]
    blocks = attention_heads(gathered.reshape(row_total, rows.shape[1]), qkv, all_labels, causal)
    own_heads, other = swap_blocks(blocks, first_id + 1, shards)
    own_heads = own_heads.reshape(rows.shape[1], rows.shape[0])

    def project(part):
        flat = part.reshape(N_Z * N_X * SHARD_PAD, rows.shape[1])
        return jnp.dot(flat, own_heads, preferred_element_type=jnp.float32)

    here, there = project(shards), project(other)
    first = lax.rem(lax.axis_index("grp"), 2) == 0
    both = jnp.stack([jnp.where(first, here, there), jnp.where(first, there, here)])
    both = both.reshape(2, N_Z, N_X, SHARD_PAD, rows.shape[0])[:, :, :, :SHARD]
    projected = both.transpose(4, 2, 1, 0, 3).reshape(rows.shape)
    return (rows.astype(jnp.float32) + projected).astype(jnp.bfloat16)


def per_device(
    patches, pictures, vis_qkv, vis_out, merge_w, text, places, segments, txt_qkv, txt_out
):
    tp_count = lax.axis_size("tp")
    grp_count = lax.axis_size("grp")
    width = patches.shape[1]
    vis_hidden = attention_layer(patches, pictures, vis_qkv, vis_out, False, 0)
    merged = layer_norm(vis_hidden).reshape(patches.shape[0] // 4, 4 * width)
    row_total = places.shape[0]
    image_parts = merge_rows(merged, merge_w, 2)
    image_rows = image_parts.transpose(1, 0, 2).reshape(row_total, width)
    tok_count = text.shape[0]
    group_tokens = tok_count * tp_count
    dest_group = places // group_tokens
    dest_local = places % tok_count
    row_ids = jnp.arange(row_total, dtype=jnp.int32)
    earlier = row_ids[:, None] > row_ids[None, :]
    same_dest = dest_group[:, None] == dest_group[None, :]
    slot_rank = jnp.sum((earlier & same_dest).astype(jnp.int32), axis=1)
    slot_index = dest_group * SEND_CAP + slot_rank
    slot_ids = jnp.arange(grp_count * SEND_CAP, dtype=jnp.int32)
    slot_pick = (slot_ids[:, None] == slot_index[None, :]).astype(jnp.bfloat16)
    marks = jnp.broadcast_to((dest_local + 1)[:, None], (row_total, LANES)).astype(jnp.bfloat16)
    send_rows = jnp.dot(
        slot_pick,
        jnp.concatenate([image_rows, marks], axis=1),
        preferred_element_type=jnp.float32,
    ).astype(jnp.bfloat16)
    send_rows = send_rows.reshape(grp_count, SEND_CAP, width + LANES)
    recv = lax.all_to_all(send_rows, "grp", split_axis=0, concat_axis=0, tiled=True)
    recv = recv.reshape(grp_count * SEND_CAP, width + LANES)
    recv_rows = recv[:, :width]
    recv_pos = recv[:, width].astype(jnp.int32) - 1
    position_hit = jnp.arange(tok_count, dtype=jnp.int32)[:, None] == recv_pos[None, :]
    placed = jnp.dot(
        position_hit.astype(jnp.bfloat16), recv_rows, preferred_element_type=jnp.float32
    ).astype(jnp.bfloat16)
    covered = jnp.any(position_hit, axis=1)
    prompt = jnp.where(covered[:, None], placed, text)
    return attention_layer(prompt, segments, txt_qkv, txt_out, True, 4)


def solution(mesh):
    placed = (
        P(("grp", "tp"), None),
        P("grp", "tp"),
        P(None, "tp", None),
        P(None, "grp"),
        P("tp", None),
        P(("grp", "tp"), None),
        P(("grp", "tp")),
        P("grp", "tp"),
        P(None, "tp", None),
        P(None, "grp"),
    )
    return jax.shard_map(
        per_device, mesh=mesh, in_specs=placed, out_specs=P(("grp", "tp"), None), check_vma=False
    )
```

```python
import functools

import jax
import jax.numpy as jnp
from jax import lax
from jax.experimental import pallas as pl
from jax.experimental.pallas import tpu as pltpu
from jax.sharding import PartitionSpec as P

HEAD_DIM = 80
SEND_CAP = 2
N_TP = 8
N_Z = 8
N_X = 4
SHARD = 20
SHARD_PAD = 24
LANES = 128


EPSILON = 1e-05
MASKED = -1e30
MESH = pl.DeviceIdType.MESH


def layer_norm(rows):
    widened = rows.astype(jnp.float32)
    row_mean = jnp.mean(widened, axis=-1, keepdims=True)
    centred = widened - row_mean
    spread = jnp.mean(centred * centred, axis=-1, keepdims=True)
    return (centred * lax.rsqrt(spread + EPSILON)).astype(jnp.bfloat16)


def times_transpose(left, right):
    return lax.dot_general(
        left, right, (((1,), (1,)), ((), ())), preferred_element_type=jnp.float32
    )


def wrap(value, count):
    return lax.rem(value + count, count)


def greet(devices):
    barrier = pltpu.get_barrier_semaphore()
    for device in devices:
        pl.semaphore_signal(barrier, inc=1, device_id=device, device_id_type=MESH)
    pl.semaphore_wait(barrier, len(devices))


Q_BLOCK = 256


def attend(qv, keys, label_rows, store, causal):
    heads_here, row_count = keys.shape[:2]
    factor = HEAD_DIM ** (-0.5) * 1.4426950408889634
    key_labels = jnp.concatenate(
        [jnp.broadcast_to(label, (LANES, LANES)).T for label in label_rows], axis=0
    )
    lanes_per = Q_BLOCK // LANES
    for block in range(row_count // Q_BLOCK):
        first = block * Q_BLOCK
        targets = range(block * lanes_per, (block + 1) * lanes_per)
        end_key = first + Q_BLOCK if causal else row_count
        allowed = jnp.concatenate(
            [key_labels[:end_key] == label_rows[target] for target in targets], axis=1
        )
        if causal:
            key_ids = lax.broadcasted_iota(jnp.int32, (end_key, Q_BLOCK), 0)
            query_ids = lax.broadcasted_iota(jnp.int32, (end_key, Q_BLOCK), 1) + first
            allowed = allowed & (query_ids >= key_ids)
        for head in range(heads_here):
            here = slice(head * HEAD_DIM, (head + 1) * HEAD_DIM)
            after = (heads_here + head) * HEAD_DIM
            queries = jnp.concatenate([qv[target, here, :] for target in targets], axis=1)
            values = jnp.concatenate(
                [qv[part, after : after + HEAD_DIM, :] for part in range(end_key // LANES)],
                axis=1,
            )
            scores = jnp.dot(
                keys[head, :end_key, :], queries, preferred_element_type=jnp.float32
            )
            scores = jnp.where(allowed, scores, MASKED)
            top = jnp.max(scores, axis=0, keepdims=True)
            weights = jnp.exp2((scores - top) * factor)
            total = jnp.sum(weights, axis=0, keepdims=True)
            mixed = jnp.dot(
                values, weights.astype(jnp.bfloat16), preferred_element_type=jnp.float32
            )
            store(targets, here, (mixed / total).astype(jnp.bfloat16))
        yield targets


def layer_kernel(causal, *refs):
    own, own_label, own_shard, weights_hbm, received, shards, other = refs[:7]
    slots, labels, weights, qv, keys, heads = refs[7:13]
    row_send, row_recv, lab_send, lab_recv, z_send, z_recv = refs[13:19]
    x_send, x_recv, core_send, core_recv, head_send, head_recv, local_sem = refs[19:]
    tp = lax.axis_index("tp")
    grp = lax.axis_index("grp")
    core = lax.rem(grp, 2)
    z_here = lax.rem(grp // 2, N_Z)
    x_here = grp // (2 * N_Z)
    half = own.shape[0] // 2
    features = heads.shape[1]

    def at_xz(x, z):
        return {"grp": (x * N_Z + z) * 2 + core}

    partner = {"grp": grp + 1 - 2 * core}
    tp_next = [{"tp": wrap(tp + 1, N_TP)}, {"tp": wrap(tp - 1, N_TP)}]
    z_next = [at_xz(x_here, wrap(z_here + 1, N_Z)), at_xz(x_here, wrap(z_here - 1, N_Z))]
    x_peers = [at_xz(wrap(x_here + d, N_X), z_here) for d in range(1, N_X)]

    fetch = pltpu.make_async_copy(weights_hbm, weights, local_sem.at[0])
    fetch.start()
    own_place = shards.at[z_here, x_here]
    keep_shard = pltpu.make_async_copy(own_shard, own_place, local_sem.at[1])
    keep_shard.start()
    slots[tp] = layer_norm(own[...])
    labels[tp] = own_label[...]
    greet([{"tp": wrap(tp + d, N_TP)} for d in range(1, N_TP)] + z_next + x_peers + [partner])

    pending = []

    def send(src, dst, send_sem, recv_sem, device):
        copy = pltpu.make_async_remote_copy(
            src_ref=src,
            dst_ref=dst,
            send_sem=send_sem,
            recv_sem=recv_sem,
            device_id=device,
            device_id_type=MESH,
        )
        copy.start()
        pending.append(copy)
        return copy

    def block_of(way, step):
        return wrap(tp - step, N_TP) if way == 0 else wrap(tp + step, N_TP)

    def z_block(way, step):
        return wrap(z_here - step, N_Z) if way == 0 else wrap(z_here + step, N_Z)

    def row_copy(way, step, part):
        place = slots.at[block_of(way, step), pl.ds(part * half, half)]
        slot = (way * 4 + step) * 2 + part
        return send(place, place, row_send.at[slot], row_recv.at[slot], tp_next[way])

    def label_copy(way, step):
        place = labels.at[block_of(way, step)]
        slot = way * 4 + step
        return send(place, place, lab_send.at[slot], lab_recv.at[slot], tp_next[way])

    def shard_copy(way, step, part):
        place = shards.at[z_block(way, step), pl.ds(part * 2, 2)]
        slot = (way * 4 + step) * 2 + part
        return send(place, place, z_send.at[slot], z_recv.at[slot], z_next[way])

    core_copies = []

    def core_copy(way, step):
        block = z_block(way, step)
        slot = way * 5 + step
        core_copies.append(
            send(shards.at[block], other.at[block], core_send.at[slot], core_recv.at[slot], partner)
        )

    def project(block):
        found = lax.dot_general(
            weights[...],
            slots[block],
            (((1,), (1,)), ((), ())),
            preferred_element_type=jnp.float32,
        )
        qv[block, :features, :] = found[:features].astype(jnp.bfloat16)
        qv[block, features:, :] = found[2 * features :].astype(jnp.bfloat16)
        place = pl.ds(pl.multiple_of(block * LANES, LANES), LANES)
        for head in range(features // HEAD_DIM):
            begin = features + head * HEAD_DIM
            keys[head, place, :] = found[begin : begin + HEAD_DIM].T.astype(jnp.bfloat16)

    row_ring, label_ring, shard_ring = {}, {}, {}
    for part in range(2):
        for way in range(2):
            row_ring[way, 0, part] = row_copy(way, 0, part)
    for way in range(2):
        label_ring[way, 0] = label_copy(way, 0)
    x_copies = [
        send(own_shard, own_place, x_send.at[d], x_recv.at[d], x_peers[d]) for d in range(N_X - 1)
    ]
    fetch.wait()
    project(tp)
    keep_shard.wait()
    for copy in x_copies:
        copy.wait_recv()
    for part in range(2):
        for way in range(2):
            shard_ring[way, 0, part] = shard_copy(way, 0, part)
    core_copy(0, 0)
    for step in range(1, 4):
        for part in range(2):
            for way in range(2):
                row_ring[way, step - 1, part].wait_recv()
                if step < 3 or part == way:
                    row_ring[way, step, part] = row_copy(way, step, part)
        for way in range(2):
            label_ring[way, step - 1].wait_recv()
            if step < 3 or way == 0:
                label_ring[way, step] = label_copy(way, step)
        for part in range(2):
            for way in range(2):
                shard_ring[way, step - 1, part].wait_recv()
                if step < 3 or part == way:
                    shard_ring[way, step, part] = shard_copy(way, step, part)
        for way in range(2):
            core_copy(way, step)
        for way in range(2):
            project(block_of(way, step))
    for way in range(2):
        row_ring[way, 3, way].wait_recv()
    label_ring[0, 3].wait_recv()
    project(block_of(0, 4))
    for way in range(2):
        shard_ring[way, 3, way].wait_recv()
    core_copy(0, 4)

    def store(targets, here, mixed):
        for index, target in enumerate(targets):
            heads[target, here, :] = mixed[:, index * LANES : (index + 1) * LANES]

    def head_copy(target):
        return pltpu.make_async_remote_copy(
            src_ref=heads.at[target],
            dst_ref=received.at[tp],
            send_sem=head_send.at[target],
            recv_sem=head_recv.at[tp],
            device_id={"tp": target},
            device_id_type=MESH,
        )

    keep_heads = pltpu.make_async_copy(heads.at[tp], received.at[tp], local_sem.at[2])
    label_rows = [labels[part].astype(jnp.float32) for part in range(N_TP)]
    for targets in attend(qv, keys, label_rows, store, causal):
        for target in targets:

            @pl.when(tp != target)
            def _():
                head_copy(target).start()

    keep_heads.start()
    keep_heads.wait()
    for target in range(N_TP):

        @pl.when(tp != target)
        def _():
            arrival = pltpu.make_async_remote_copy(
                src_ref=heads.at[target],
                dst_ref=received.at[target],
                send_sem=head_send.at[target],
                recv_sem=head_recv.at[target],
                device_id={"tp": target},
                device_id_type=MESH,
            )
            arrival.wait_send()
            arrival.wait_recv()

    for copy in core_copies:
        copy.wait_recv()
    for copy in pending:
        copy.wait_send()


def run_layer(rows, labels, qkv, shard, causal, collective_id):
    row_total, width = rows.shape
    features = qkv.shape[1]
    weights = qkv.reshape(3 * features, width)
    vmem = pl.BlockSpec(memory_space=pltpu.VMEM)
    hbm = pl.BlockSpec(memory_space=pl.ANY)
    dma = pltpu.SemaphoreType.DMA
    bf16 = jnp.bfloat16
    all_shards = jax.ShapeDtypeStruct((N_Z, N_X, *shard.shape), bf16)
    return pl.pallas_call(
        functools.partial(layer_kernel, causal),
        out_shape=[
            jax.ShapeDtypeStruct((N_TP, features, row_total), bf16),
            all_shards,
            all_shards,
        ],
        in_specs=[vmem, vmem, vmem, hbm],
        out_specs=[hbm] * 3,
        scratch_shapes=[
            pltpu.VMEM((N_TP, row_total, width), bf16),
            pltpu.VMEM((N_TP, *labels.shape), labels.dtype),
            pltpu.VMEM(weights.shape, bf16),
            pltpu.VMEM((N_TP, 2 * features, row_total), bf16),
            pltpu.VMEM((features // HEAD_DIM, N_TP * row_total, HEAD_DIM), bf16),
            pltpu.VMEM((N_TP, features, row_total), bf16),
            dma((16,)),
            dma((16,)),
            dma((8,)),
            dma((8,)),
            dma((16,)),
            dma((16,)),
            dma((3,)),
            dma((3,)),
            dma((10,)),
            dma((10,)),
            dma((8,)),
            dma((8,)),
            dma((3,)),
        ],
        compiler_params=pltpu.CompilerParams(collective_id=collective_id, has_side_effects=True),
    )(rows, labels, shard, weights)


def merge_kernel(own, weights_hbm, image, slots, weights, results, *sems):
    row_send, row_recv, col_send, col_recv, local_sem = sems
    tp = lax.axis_index("tp")
    half = own.shape[0] // 2
    greet([{"tp": wrap(tp + d, N_TP)} for d in range(1, N_TP)])
    neighbours = [{"tp": wrap(tp + 1, N_TP)}, {"tp": wrap(tp - 1, N_TP)}]

    def block_of(way, step):
        return wrap(tp - step, N_TP) if way == 0 else wrap(tp + step, N_TP)

    def row_copy(way, step, part):
        span = pl.ds(part * half, half)
        dst = slots.at[block_of(way, step), span]
        slot = (way * 4 + step) * 2 + part
        return pltpu.make_async_remote_copy(
            src_ref=own.at[span] if step == 0 else dst,
            dst_ref=dst,
            send_sem=row_send.at[slot],
            recv_sem=row_recv.at[slot],
            device_id=neighbours[way],
            device_id_type=MESH,
        )

    pending = []
    ring = {}

    def start(way, step, part):
        ring[way, step, part] = row_copy(way, step, part)
        ring[way, step, part].start()
        pending.append(ring[way, step, part])

    for part in range(2):
        for way in range(2):
            start(way, 0, part)
    fetch = pltpu.make_async_copy(weights_hbm, weights, local_sem.at[0])
    fetch.start()
    fetch.wait()

    def columns(block):
        return times_transpose(block, weights[...]).astype(jnp.bfloat16)

    results[tp] = columns(own[...])
    keep = pltpu.make_async_copy(results.at[tp], image.at[tp], local_sem.at[1])
    keep.start()
    arrivals = []

    def give(way, step):
        block = block_of(way, step)
        results[block] = columns(slots[block])
        copy = pltpu.make_async_remote_copy(
            src_ref=results.at[block],
            dst_ref=image.at[tp],
            send_sem=col_send.at[way * 5 + step],
            recv_sem=col_recv.at[way * 5 + step],
            device_id={"tp": block},
            device_id_type=MESH,
        )
        copy.start()
        pending.append(copy)
        arrivals.append(copy)

    for step in range(1, 4):
        for part in range(2):
            for way in range(2):
                ring[way, step - 1, part].wait_recv()
                if step < 3 or part == way:
                    start(way, step, part)
        for way in range(2):
            give(way, step)
    for way in range(2):
        ring[way, 3, way].wait_recv()
    give(0, 4)
    keep.wait()
    for copy in arrivals:
        copy.wait_recv()
    for copy in pending:
        copy.wait_send()


def merge_rows(merged, merge_w, collective_id):
    row_total, depth = merged.shape
    features = merge_w.shape[0]
    hbm = pl.BlockSpec(memory_space=pl.ANY)
    dma = pltpu.SemaphoreType.DMA
    return pl.pallas_call(
        merge_kernel,
        out_shape=jax.ShapeDtypeStruct((N_TP, row_total, features), jnp.bfloat16),
        in_specs=[pl.BlockSpec(memory_space=pltpu.VMEM), hbm],
        out_specs=hbm,
        scratch_shapes=[
            pltpu.VMEM((N_TP, row_total, depth), jnp.bfloat16),
            pltpu.VMEM((features, depth), jnp.bfloat16),
            pltpu.VMEM((N_TP, row_total, features), jnp.bfloat16),
            dma((16,)),
            dma((16,)),
            dma((10,)),
            dma((10,)),
            dma((2,)),
        ],
        compiler_params=pltpu.CompilerParams(collective_id=collective_id, has_side_effects=True),
    )(merged, merge_w)


def attention_layer(rows, labels, qkv, columns, causal, first_id):
    shard = jnp.pad(columns.T, ((0, SHARD_PAD - SHARD), (0, 0)))
    own_heads, shards, other = run_layer(rows, labels, qkv, shard, causal, first_id)
    own_heads = own_heads.reshape(rows.shape[1], rows.shape[0])

    def project(part):
        flat = part.reshape(N_Z * N_X * SHARD_PAD, rows.shape[1])
        return jnp.dot(flat, own_heads, preferred_element_type=jnp.float32)

    here, there = project(shards), project(other)
    first = lax.rem(lax.axis_index("grp"), 2) == 0
    both = jnp.stack([jnp.where(first, here, there), jnp.where(first, there, here)])
    both = both.reshape(2, N_Z, N_X, SHARD_PAD, rows.shape[0])[:, :, :, :SHARD]
    projected = both.transpose(4, 2, 1, 0, 3).reshape(rows.shape)
    return (rows.astype(jnp.float32) + projected).astype(jnp.bfloat16)


def per_device(
    patches, pictures, vis_qkv, vis_out, merge_w, text, places, segments, txt_qkv, txt_out
):
    tp_count = lax.axis_size("tp")
    grp_count = lax.axis_size("grp")
    width = patches.shape[1]
    vis_hidden = attention_layer(patches, pictures, vis_qkv, vis_out, False, 0)
    merged = layer_norm(vis_hidden).reshape(patches.shape[0] // 4, 4 * width)
    row_total = places.shape[0]
    image_parts = merge_rows(merged, merge_w, 2)
    image_rows = image_parts.transpose(1, 0, 2).reshape(row_total, width)
    tok_count = text.shape[0]
    group_tokens = tok_count * tp_count
    dest_group = places // group_tokens
    dest_local = places % tok_count
    row_ids = jnp.arange(row_total, dtype=jnp.int32)
    earlier = row_ids[:, None] > row_ids[None, :]
    same_dest = dest_group[:, None] == dest_group[None, :]
    slot_rank = jnp.sum((earlier & same_dest).astype(jnp.int32), axis=1)
    slot_index = dest_group * SEND_CAP + slot_rank
    slot_ids = jnp.arange(grp_count * SEND_CAP, dtype=jnp.int32)
    slot_pick = (slot_ids[:, None] == slot_index[None, :]).astype(jnp.bfloat16)
    marks = jnp.broadcast_to((dest_local + 1)[:, None], (row_total, LANES)).astype(jnp.bfloat16)
    send_rows = jnp.dot(
        slot_pick,
        jnp.concatenate([image_rows, marks], axis=1),
        preferred_element_type=jnp.float32,
    ).astype(jnp.bfloat16)
    send_rows = send_rows.reshape(grp_count, SEND_CAP, width + LANES)
    recv = lax.all_to_all(send_rows, "grp", split_axis=0, concat_axis=0, tiled=True)
    recv = recv.reshape(grp_count * SEND_CAP, width + LANES)
    recv_rows = recv[:, :width]
    recv_pos = recv[:, width].astype(jnp.int32) - 1
    position_hit = jnp.arange(tok_count, dtype=jnp.int32)[:, None] == recv_pos[None, :]
    placed = jnp.dot(
        position_hit.astype(jnp.bfloat16), recv_rows, preferred_element_type=jnp.float32
    ).astype(jnp.bfloat16)
    covered = jnp.any(position_hit, axis=1)
    prompt = jnp.where(covered[:, None], placed, text)
    return attention_layer(prompt, segments, txt_qkv, txt_out, True, 4)


def solution(mesh):
    placed = (
        P(("grp", "tp"), None),
        P("grp", "tp"),
        P(None, "tp", None),
        P(None, "grp"),
        P("tp", None),
        P(("grp", "tp"), None),
        P(("grp", "tp")),
        P("grp", "tp"),
        P(None, "tp", None),
        P(None, "grp"),
    )
    return jax.shard_map(
        per_device, mesh=mesh, in_specs=placed, out_specs=P(("grp", "tp"), None), check_vma=False
    )
```

```python
import functools

import jax
import jax.numpy as jnp
from jax import lax
from jax.experimental import pallas as pl
from jax.experimental.pallas import tpu as pltpu
from jax.sharding import PartitionSpec as P

HEAD_DIM = 80
SEND_CAP = 2
N_TP = 8
N_Z = 8
N_X = 4
SHARD = 20
SHARD_PAD = 24
LANES = 128


EPSILON = 1e-05
MASKED = -1e30
MESH = pl.DeviceIdType.MESH


def layer_norm(rows):
    widened = rows.astype(jnp.float32)
    row_mean = jnp.mean(widened, axis=-1, keepdims=True)
    centred = widened - row_mean
    spread = jnp.mean(centred * centred, axis=-1, keepdims=True)
    return (centred * lax.rsqrt(spread + EPSILON)).astype(jnp.bfloat16)


def times_transpose(left, right):
    return lax.dot_general(
        left, right, (((1,), (1,)), ((), ())), preferred_element_type=jnp.float32
    )


def wrap(value, count):
    return lax.rem(value + count, count)


def greet(devices):
    barrier = pltpu.get_barrier_semaphore()
    for device in devices:
        pl.semaphore_signal(barrier, inc=1, device_id=device, device_id_type=MESH)
    pl.semaphore_wait(barrier, len(devices))


Q_BLOCK = 256


def attend(qv, keys, label_rows, store, causal):
    heads_here, row_count = keys.shape[:2]
    factor = HEAD_DIM ** (-0.5) * 1.4426950408889634
    key_labels = jnp.concatenate(
        [jnp.broadcast_to(label, (LANES, LANES)).T for label in label_rows], axis=0
    )
    lanes_per = Q_BLOCK // LANES
    for block in range(row_count // Q_BLOCK):
        first = block * Q_BLOCK
        targets = range(block * lanes_per, (block + 1) * lanes_per)
        end_key = first + Q_BLOCK if causal else row_count
        allowed = jnp.concatenate(
            [key_labels[:end_key] == label_rows[target] for target in targets], axis=1
        )
        if causal:
            key_ids = lax.broadcasted_iota(jnp.int32, (end_key, Q_BLOCK), 0)
            query_ids = lax.broadcasted_iota(jnp.int32, (end_key, Q_BLOCK), 1) + first
            allowed = allowed & (query_ids >= key_ids)
        for head in range(heads_here):
            here = slice(head * HEAD_DIM, (head + 1) * HEAD_DIM)
            after = (heads_here + head) * HEAD_DIM
            queries = jnp.concatenate([qv[target, here, :] for target in targets], axis=1)
            values = jnp.concatenate(
                [qv[part, after : after + HEAD_DIM, :] for part in range(end_key // LANES)],
                axis=1,
            )
            scores = jnp.dot(
                keys[head, :end_key, :], queries, preferred_element_type=jnp.float32
            )
            scores = jnp.where(allowed, scores, MASKED)
            top = jnp.max(scores, axis=0, keepdims=True)
            weights = jnp.exp2((scores - top) * factor)
            total = jnp.sum(weights, axis=0, keepdims=True)
            mixed = jnp.dot(
                values, weights.astype(jnp.bfloat16), preferred_element_type=jnp.float32
            )
            store(targets, here, (mixed / total).astype(jnp.bfloat16))
        yield targets


def layer_kernel(causal, *refs):
    own, own_label, columns, weights_hbm, received, shards, other = refs[:7]
    slots, labels, weights, qv, keys, heads, own_shard = refs[7:14]
    row_send, row_recv, lab_send, lab_recv, z_send, z_recv = refs[14:20]
    x_send, x_recv, core_send, core_recv, head_send, head_recv, local_sem = refs[20:]
    tp = lax.axis_index("tp")
    grp = lax.axis_index("grp")
    core = lax.rem(grp, 2)
    z_here = lax.rem(grp // 2, N_Z)
    x_here = grp // (2 * N_Z)
    half = own.shape[0] // 2
    features = heads.shape[1]

    def at_xz(x, z):
        return {"grp": (x * N_Z + z) * 2 + core}

    partner = {"grp": grp + 1 - 2 * core}
    tp_next = [{"tp": wrap(tp + 1, N_TP)}, {"tp": wrap(tp - 1, N_TP)}]
    z_next = [at_xz(x_here, wrap(z_here + 1, N_Z)), at_xz(x_here, wrap(z_here - 1, N_Z))]
    x_peers = [at_xz(wrap(x_here + d, N_X), z_here) for d in range(1, N_X)]

    fetch = pltpu.make_async_copy(weights_hbm, weights, local_sem.at[0])
    fetch.start()
    own_place = shards.at[z_here, x_here]
    own_shard[...] = jnp.zeros_like(own_shard)
    own_shard[: columns.shape[0], :] = columns[...]
    slots[tp] = layer_norm(own[...])
    labels[tp] = own_label[...]
    greet([{"tp": wrap(tp + d, N_TP)} for d in range(1, N_TP)] + z_next + x_peers + [partner])

    pending = []

    def send(src, dst, send_sem, recv_sem, device):
        copy = pltpu.make_async_remote_copy(
            src_ref=src,
            dst_ref=dst,
            send_sem=send_sem,
            recv_sem=recv_sem,
            device_id=device,
            device_id_type=MESH,
        )
        copy.start()
        pending.append(copy)
        return copy

    def block_of(way, step):
        return wrap(tp - step, N_TP) if way == 0 else wrap(tp + step, N_TP)

    def z_block(way, step):
        return wrap(z_here - step, N_Z) if way == 0 else wrap(z_here + step, N_Z)

    def row_copy(way, step, part):
        place = slots.at[block_of(way, step), pl.ds(part * half, half)]
        slot = (way * 4 + step) * 2 + part
        return send(place, place, row_send.at[slot], row_recv.at[slot], tp_next[way])

    def label_copy(way, step):
        place = labels.at[block_of(way, step)]
        slot = way * 4 + step
        return send(place, place, lab_send.at[slot], lab_recv.at[slot], tp_next[way])

    def shard_copy(way, step, part):
        place = shards.at[z_block(way, step), pl.ds(part * 2, 2)]
        slot = (way * 4 + step) * 2 + part
        return send(place, place, z_send.at[slot], z_recv.at[slot], z_next[way])

    core_copies = []

    def core_copy(way, step):
        block = z_block(way, step)
        slot = way * 5 + step
        core_copies.append(
            send(shards.at[block], other.at[block], core_send.at[slot], core_recv.at[slot], partner)
        )

    def project(block):
        found = lax.dot_general(
            weights[...],
            slots[block],
            (((1,), (1,)), ((), ())),
            preferred_element_type=jnp.float32,
        )
        qv[block, :features, :] = found[:features].astype(jnp.bfloat16)
        qv[block, features:, :] = found[2 * features :].astype(jnp.bfloat16)
        place = pl.ds(pl.multiple_of(block * LANES, LANES), LANES)
        for head in range(features // HEAD_DIM):
            begin = features + head * HEAD_DIM
            keys[head, place, :] = found[begin : begin + HEAD_DIM].T.astype(jnp.bfloat16)

    row_ring, label_ring, shard_ring = {}, {}, {}
    for part in range(2):
        for way in range(2):
            row_ring[way, 0, part] = row_copy(way, 0, part)
    for way in range(2):
        label_ring[way, 0] = label_copy(way, 0)
    x_copies = [
        send(own_shard, own_place, x_send.at[d], x_recv.at[d], x_peers[d]) for d in range(N_X - 1)
    ]
    keep_shard = pltpu.make_async_copy(own_shard, own_place, local_sem.at[1])
    keep_shard.start()
    fetch.wait()
    project(tp)

    def shard_step(step):
        if step == 0:
            keep_shard.wait()
            for copy in x_copies:
                copy.wait_recv()
        for part in range(2):
            for way in range(2):
                if step and (step < 4 or part == way):
                    shard_ring[way, step - 1, part].wait_recv()
                if step < 3 or (step == 3 and part == way):
                    shard_ring[way, step, part] = shard_copy(way, step, part)
        for way in range(2 if step in (1, 2, 3) else 1):
            core_copy(way, step)

    for step in range(1, 4):
        for part in range(2):
            for way in range(2):
                row_ring[way, step - 1, part].wait_recv()
                if step < 3 or part == way:
                    row_ring[way, step, part] = row_copy(way, step, part)
        for way in range(2):
            label_ring[way, step - 1].wait_recv()
            if step < 3 or way == 0:
                label_ring[way, step] = label_copy(way, step)
        for way in range(2):
            project(block_of(way, step))
        shard_step(step - 1)
    for way in range(2):
        row_ring[way, 3, way].wait_recv()
    label_ring[0, 3].wait_recv()
    project(block_of(0, 4))
    def store(targets, here, mixed):
        for index, target in enumerate(targets):
            heads[target, here, :] = mixed[:, index * LANES : (index + 1) * LANES]

    def head_copy(target):
        return pltpu.make_async_remote_copy(
            src_ref=heads.at[target],
            dst_ref=received.at[tp],
            send_sem=head_send.at[target],
            recv_sem=head_recv.at[tp],
            device_id={"tp": target},
            device_id_type=MESH,
        )

    keep_heads = pltpu.make_async_copy(heads.at[tp], received.at[tp], local_sem.at[2])
    label_rows = [labels[part].astype(jnp.float32) for part in range(N_TP)]
    for done, targets in enumerate(attend(qv, keys, label_rows, store, causal)):
        if done < 2:
            shard_step(3 + done)
        for target in targets:

            @pl.when(tp != target)
            def _():
                head_copy(target).start()

    keep_heads.start()
    keep_heads.wait()
    for target in range(N_TP):

        @pl.when(tp != target)
        def _():
            arrival = pltpu.make_async_remote_copy(
                src_ref=heads.at[target],
                dst_ref=received.at[target],
                send_sem=head_send.at[target],
                recv_sem=head_recv.at[target],
                device_id={"tp": target},
                device_id_type=MESH,
            )
            arrival.wait_send()
            arrival.wait_recv()

    for copy in core_copies:
        copy.wait_recv()
    for copy in pending:
        copy.wait_send()


def run_layer(rows, labels, qkv, shard, causal, collective_id):
    row_total, width = rows.shape
    features = qkv.shape[1]
    weights = qkv.reshape(3 * features, width)
    vmem = pl.BlockSpec(memory_space=pltpu.VMEM)
    hbm = pl.BlockSpec(memory_space=pl.ANY)
    dma = pltpu.SemaphoreType.DMA
    bf16 = jnp.bfloat16
    all_shards = jax.ShapeDtypeStruct((N_Z, N_X, SHARD_PAD, width), bf16)
    return pl.pallas_call(
        functools.partial(layer_kernel, causal),
        out_shape=[
            jax.ShapeDtypeStruct((N_TP, features, row_total), bf16),
            all_shards,
            all_shards,
        ],
        in_specs=[vmem, vmem, vmem, hbm],
        out_specs=[hbm] * 3,
        scratch_shapes=[
            pltpu.VMEM((N_TP, row_total, width), bf16),
            pltpu.VMEM((N_TP, *labels.shape), labels.dtype),
            pltpu.VMEM(weights.shape, bf16),
            pltpu.VMEM((N_TP, 2 * features, row_total), bf16),
            pltpu.VMEM((features // HEAD_DIM, N_TP * row_total, HEAD_DIM), bf16),
            pltpu.VMEM((N_TP, features, row_total), bf16),
            pltpu.VMEM((SHARD_PAD, width), bf16),
            dma((16,)),
            dma((16,)),
            dma((8,)),
            dma((8,)),
            dma((16,)),
            dma((16,)),
            dma((3,)),
            dma((3,)),
            dma((10,)),
            dma((10,)),
            dma((8,)),
            dma((8,)),
            dma((3,)),
        ],
        compiler_params=pltpu.CompilerParams(collective_id=collective_id, has_side_effects=True),
    )(rows, labels, shard, weights)


def merge_kernel(own, weights_hbm, out, slots, weights, results, image, *sems):
    row_send, row_recv, col_send, col_recv, local_sem = sems
    tp = lax.axis_index("tp")
    half = own.shape[0] // 2
    greet([{"tp": wrap(tp + d, N_TP)} for d in range(1, N_TP)])
    neighbours = [{"tp": wrap(tp + 1, N_TP)}, {"tp": wrap(tp - 1, N_TP)}]

    def block_of(way, step):
        return wrap(tp - step, N_TP) if way == 0 else wrap(tp + step, N_TP)

    def row_copy(way, step, part):
        span = pl.ds(part * half, half)
        dst = slots.at[block_of(way, step), span]
        slot = (way * 4 + step) * 2 + part
        return pltpu.make_async_remote_copy(
            src_ref=own.at[span] if step == 0 else dst,
            dst_ref=dst,
            send_sem=row_send.at[slot],
            recv_sem=row_recv.at[slot],
            device_id=neighbours[way],
            device_id_type=MESH,
        )

    pending = []
    ring = {}

    def start(way, step, part):
        ring[way, step, part] = row_copy(way, step, part)
        ring[way, step, part].start()
        pending.append(ring[way, step, part])

    for part in range(2):
        for way in range(2):
            start(way, 0, part)
    fetch = pltpu.make_async_copy(weights_hbm, weights, local_sem.at[0])
    fetch.start()
    fetch.wait()

    def columns(block):
        return times_transpose(block, weights[...]).astype(jnp.bfloat16)

    results[tp] = columns(own[...])
    keep = pltpu.make_async_copy(results.at[tp], image.at[tp], local_sem.at[1])
    keep.start()
    arrivals = []

    def give(way, step):
        block = block_of(way, step)
        results[block] = columns(slots[block])
        copy = pltpu.make_async_remote_copy(
            src_ref=results.at[block],
            dst_ref=image.at[tp],
            send_sem=col_send.at[way * 5 + step],
            recv_sem=col_recv.at[way * 5 + step],
            device_id={"tp": block},
            device_id_type=MESH,
        )
        copy.start()
        pending.append(copy)
        arrivals.append(copy)

    for step in range(1, 4):
        for part in range(2):
            for way in range(2):
                ring[way, step - 1, part].wait_recv()
                if step < 3 or part == way:
                    start(way, step, part)
        for way in range(2):
            give(way, step)
    for way in range(2):
        ring[way, 3, way].wait_recv()
    give(0, 4)
    keep.wait()
    for copy in arrivals:
        copy.wait_recv()
    out[...] = jnp.concatenate(
        [image[part].astype(jnp.float32) for part in range(N_TP)], axis=1
    ).astype(jnp.bfloat16)
    for copy in pending:
        copy.wait_send()


def merge_rows(merged, merge_w, collective_id):
    row_total, depth = merged.shape
    features = merge_w.shape[0]
    hbm = pl.BlockSpec(memory_space=pl.ANY)
    dma = pltpu.SemaphoreType.DMA
    return pl.pallas_call(
        merge_kernel,
        out_shape=jax.ShapeDtypeStruct((row_total, N_TP * features), jnp.bfloat16),
        in_specs=[pl.BlockSpec(memory_space=pltpu.VMEM), hbm],
        out_specs=pl.BlockSpec(memory_space=pltpu.VMEM),
        scratch_shapes=[
            pltpu.VMEM((N_TP, row_total, depth), jnp.bfloat16),
            pltpu.VMEM((features, depth), jnp.bfloat16),
            pltpu.VMEM((N_TP, row_total, features), jnp.bfloat16),
            pltpu.VMEM((N_TP, row_total, features), jnp.bfloat16),
            dma((16,)),
            dma((16,)),
            dma((10,)),
            dma((10,)),
            dma((2,)),
        ],
        compiler_params=pltpu.CompilerParams(collective_id=collective_id, has_side_effects=True),
    )(merged, merge_w)


def attention_layer(rows, labels, qkv, columns, causal, first_id):
    own_heads, shards, other = run_layer(rows, labels, qkv, columns.T, causal, first_id)
    own_heads = own_heads.reshape(rows.shape[1], rows.shape[0])

    def project(part):
        flat = part.reshape(N_Z * N_X * SHARD_PAD, rows.shape[1])
        return jnp.dot(flat, own_heads, preferred_element_type=jnp.float32)

    here, there = project(shards), project(other)
    first = lax.rem(lax.axis_index("grp"), 2) == 0
    both = jnp.stack([jnp.where(first, here, there), jnp.where(first, there, here)])
    both = both.reshape(2, N_Z, N_X, SHARD_PAD, rows.shape[0])[:, :, :, :SHARD]
    projected = both.transpose(4, 2, 1, 0, 3).reshape(rows.shape)
    return (rows.astype(jnp.float32) + projected).astype(jnp.bfloat16)


def per_device(
    patches, pictures, vis_qkv, vis_out, merge_w, text, places, segments, txt_qkv, txt_out
):
    tp_count = lax.axis_size("tp")
    grp_count = lax.axis_size("grp")
    width = patches.shape[1]
    vis_hidden = attention_layer(patches, pictures, vis_qkv, vis_out, False, 0)
    merged = layer_norm(vis_hidden).reshape(patches.shape[0] // 4, 4 * width)
    row_total = places.shape[0]
    image_rows = merge_rows(merged, merge_w, 2)
    tok_count = text.shape[0]
    group_tokens = tok_count * tp_count
    dest_group = places // group_tokens
    dest_local = places % tok_count
    row_ids = jnp.arange(row_total, dtype=jnp.int32)
    earlier = row_ids[:, None] > row_ids[None, :]
    same_dest = dest_group[:, None] == dest_group[None, :]
    slot_rank = jnp.sum((earlier & same_dest).astype(jnp.int32), axis=1)
    slot_index = dest_group * SEND_CAP + slot_rank
    slot_ids = jnp.arange(grp_count * SEND_CAP, dtype=jnp.int32)
    slot_pick = (slot_ids[:, None] == slot_index[None, :]).astype(jnp.bfloat16)
    marks = jnp.broadcast_to((dest_local + 1)[:, None], (row_total, LANES)).astype(jnp.bfloat16)
    send_rows = jnp.dot(
        slot_pick,
        jnp.concatenate([image_rows, marks], axis=1),
        preferred_element_type=jnp.float32,
    ).astype(jnp.bfloat16)
    send_rows = send_rows.reshape(grp_count, SEND_CAP, width + LANES)
    recv = lax.all_to_all(send_rows, "grp", split_axis=0, concat_axis=0, tiled=True)
    recv = recv.reshape(grp_count * SEND_CAP, width + LANES)
    recv_rows = recv[:, :width]
    recv_pos = recv[:, width].astype(jnp.int32) - 1
    position_hit = jnp.arange(tok_count, dtype=jnp.int32)[:, None] == recv_pos[None, :]
    placed = jnp.dot(
        position_hit.astype(jnp.bfloat16), recv_rows, preferred_element_type=jnp.float32
    ).astype(jnp.bfloat16)
    covered = jnp.any(position_hit, axis=1)
    prompt = jnp.where(covered[:, None], placed, text)
    return attention_layer(prompt, segments, txt_qkv, txt_out, True, 4)


def solution(mesh):
    placed = (
        P(("grp", "tp"), None),
        P("grp", "tp"),
        P(None, "tp", None),
        P(None, "grp"),
        P("tp", None),
        P(("grp", "tp"), None),
        P(("grp", "tp")),
        P("grp", "tp"),
        P(None, "tp", None),
        P(None, "grp"),
    )
    return jax.shard_map(
        per_device, mesh=mesh, in_specs=placed, out_specs=P(("grp", "tp"), None), check_vma=False
    )
```

```python
import functools

import jax
import jax.numpy as jnp
from jax import lax
from jax.experimental import pallas as pl
from jax.experimental.pallas import tpu as pltpu
from jax.sharding import PartitionSpec as P

HEAD_DIM = 80
SEND_CAP = 2
N_TP = 8
N_Z = 8
N_X = 4
SHARD = 20
SHARD_PAD = 24
LANES = 128


EPSILON = 1e-05
MASKED = -1e30
MESH = pl.DeviceIdType.MESH


def layer_norm(rows):
    widened = rows.astype(jnp.float32)
    row_mean = jnp.mean(widened, axis=-1, keepdims=True)
    centred = widened - row_mean
    spread = jnp.mean(centred * centred, axis=-1, keepdims=True)
    return (centred * lax.rsqrt(spread + EPSILON)).astype(jnp.bfloat16)


def times_transpose(left, right):
    return lax.dot_general(
        left, right, (((1,), (1,)), ((), ())), preferred_element_type=jnp.float32
    )


def wrap(value, count):
    return lax.rem(value + count, count)


def greet(devices):
    barrier = pltpu.get_barrier_semaphore()
    for device in devices:
        pl.semaphore_signal(barrier, inc=1, device_id=device, device_id_type=MESH)
    pl.semaphore_wait(barrier, len(devices))


Q_BLOCK = 256


def attend(qv, keys, label_rows, store, causal):
    heads_here, row_count = keys.shape[:2]
    factor = HEAD_DIM ** (-0.5) * 1.4426950408889634
    key_labels = jnp.concatenate(
        [jnp.broadcast_to(label, (LANES, LANES)).T for label in label_rows], axis=0
    )
    lanes_per = Q_BLOCK // LANES
    for block in range(row_count // Q_BLOCK):
        first = block * Q_BLOCK
        targets = range(block * lanes_per, (block + 1) * lanes_per)
        end_key = first + Q_BLOCK if causal else row_count
        allowed = jnp.concatenate(
            [key_labels[:end_key] == label_rows[target] for target in targets], axis=1
        )
        if causal:
            key_ids = lax.broadcasted_iota(jnp.int32, (end_key, Q_BLOCK), 0)
            query_ids = lax.broadcasted_iota(jnp.int32, (end_key, Q_BLOCK), 1) + first
            allowed = allowed & (query_ids >= key_ids)
        for head in range(heads_here):
            here = slice(head * HEAD_DIM, (head + 1) * HEAD_DIM)
            after = (heads_here + head) * HEAD_DIM
            queries = jnp.concatenate([qv[target, here, :] for target in targets], axis=1)
            values = jnp.concatenate(
                [qv[part, after : after + HEAD_DIM, :] for part in range(end_key // LANES)],
                axis=1,
            )
            scores = jnp.dot(
                keys[head, :end_key, :], queries, preferred_element_type=jnp.float32
            )
            scores = jnp.where(allowed, scores, MASKED)
            top = jnp.max(scores, axis=0, keepdims=True)
            weights = jnp.exp2((scores - top) * factor)
            total = jnp.sum(weights, axis=0, keepdims=True)
            mixed = jnp.dot(
                values, weights.astype(jnp.bfloat16), preferred_element_type=jnp.float32
            )
            store(targets, here, (mixed / total).astype(jnp.bfloat16))
        yield targets


def layer_kernel(causal, *refs):
    own, own_label, columns, weights_hbm, received, shards, other = refs[:7]
    slots, labels, weights, qv, keys, heads, own_shard = refs[7:14]
    row_send, row_recv, lab_send, lab_recv, z_send, z_recv = refs[14:20]
    x_send, x_recv, core_send, core_recv, head_send, head_recv, local_sem = refs[20:]
    tp = lax.axis_index("tp")
    grp = lax.axis_index("grp")
    core = lax.rem(grp, 2)
    z_here = lax.rem(grp // 2, N_Z)
    x_here = grp // (2 * N_Z)
    half = own.shape[0] // 2
    features = heads.shape[1]

    def at_xz(x, z):
        return {"grp": (x * N_Z + z) * 2 + core}

    partner = {"grp": grp + 1 - 2 * core}
    tp_next = [{"tp": wrap(tp + 1, N_TP)}, {"tp": wrap(tp - 1, N_TP)}]
    z_next = [at_xz(x_here, wrap(z_here + 1, N_Z)), at_xz(x_here, wrap(z_here - 1, N_Z))]
    x_peers = [at_xz(wrap(x_here + d, N_X), z_here) for d in range(1, N_X)]

    fetch = pltpu.make_async_copy(weights_hbm, weights, local_sem.at[0])
    fetch.start()
    own_place = shards.at[z_here, x_here]
    own_shard[...] = jnp.zeros_like(own_shard)
    own_shard[: columns.shape[0], :] = columns[...]
    slots[tp] = layer_norm(own[...])
    labels[tp] = own_label[...]
    greet([{"tp": wrap(tp + d, N_TP)} for d in range(1, N_TP)] + z_next + x_peers + [partner])

    pending = []

    def send(src, dst, send_sem, recv_sem, device):
        copy = pltpu.make_async_remote_copy(
            src_ref=src,
            dst_ref=dst,
            send_sem=send_sem,
            recv_sem=recv_sem,
            device_id=device,
            device_id_type=MESH,
        )
        copy.start()
        pending.append(copy)
        return copy

    def block_of(way, step):
        return wrap(tp - step, N_TP) if way == 0 else wrap(tp + step, N_TP)

    def z_block(way, step):
        return wrap(z_here - step, N_Z) if way == 0 else wrap(z_here + step, N_Z)

    def row_copy(way, step, part):
        place = slots.at[block_of(way, step), pl.ds(part * half, half)]
        slot = (way * 4 + step) * 2 + part
        return send(place, place, row_send.at[slot], row_recv.at[slot], tp_next[way])

    def label_copy(way, step):
        place = labels.at[block_of(way, step)]
        slot = way * 4 + step
        return send(place, place, lab_send.at[slot], lab_recv.at[slot], tp_next[way])

    def shard_copy(way, step, part):
        place = shards.at[z_block(way, step), pl.ds(part * 2, 2)]
        slot = (way * 4 + step) * 2 + part
        return send(place, place, z_send.at[slot], z_recv.at[slot], z_next[way])

    core_copies = []

    def core_copy(way, step):
        block = z_block(way, step)
        slot = way * 5 + step
        core_copies.append(
            send(shards.at[block], other.at[block], core_send.at[slot], core_recv.at[slot], partner)
        )

    def project(block):
        found = lax.dot_general(
            weights[...],
            slots[block],
            (((1,), (1,)), ((), ())),
            preferred_element_type=jnp.float32,
        )
        qv[block, :features, :] = found[:features].astype(jnp.bfloat16)
        qv[block, features:, :] = found[2 * features :].astype(jnp.bfloat16)
        place = pl.ds(pl.multiple_of(block * LANES, LANES), LANES)
        for head in range(features // HEAD_DIM):
            begin = features + head * HEAD_DIM
            keys[head, place, :] = found[begin : begin + HEAD_DIM].T.astype(jnp.bfloat16)

    row_ring, label_ring, shard_ring = {}, {}, {}
    for part in range(2):
        for way in range(2):
            row_ring[way, 0, part] = row_copy(way, 0, part)
    for way in range(2):
        label_ring[way, 0] = label_copy(way, 0)
    x_copies = [
        send(own_shard, own_place, x_send.at[d], x_recv.at[d], x_peers[d]) for d in range(N_X - 1)
    ]
    keep_shard = pltpu.make_async_copy(own_shard, own_place, local_sem.at[1])
    keep_shard.start()
    fetch.wait()
    project(tp)

    def shard_step(step):
        if step == 0:
            keep_shard.wait()
            for copy in x_copies:
                copy.wait_recv()
        for part in range(2):
            for way in range(2):
                if step and (step < 4 or part == way):
                    shard_ring[way, step - 1, part].wait_recv()
                if step < 3 or (step == 3 and part == way):
                    shard_ring[way, step, part] = shard_copy(way, step, part)
        for way in range(2 if step in (1, 2, 3) else 1):
            core_copy(way, step)

    shard_step(0)
    for step in range(1, 4):
        for part in range(2):
            for way in range(2):
                row_ring[way, step - 1, part].wait_recv()
                if step < 3 or part == way:
                    row_ring[way, step, part] = row_copy(way, step, part)
        for way in range(2):
            label_ring[way, step - 1].wait_recv()
            if step < 3 or way == 0:
                label_ring[way, step] = label_copy(way, step)
        for way in range(2):
            project(block_of(way, step))
        shard_step(step)
    for way in range(2):
        row_ring[way, 3, way].wait_recv()
    label_ring[0, 3].wait_recv()
    project(block_of(0, 4))
    shard_step(4)
    def store(targets, here, mixed):
        for index, target in enumerate(targets):
            heads[target, here, :] = mixed[:, index * LANES : (index + 1) * LANES]

    def head_copy(target):
        return pltpu.make_async_remote_copy(
            src_ref=heads.at[target],
            dst_ref=received.at[tp],
            send_sem=head_send.at[target],
            recv_sem=head_recv.at[tp],
            device_id={"tp": target},
            device_id_type=MESH,
        )

    keep_heads = pltpu.make_async_copy(heads.at[tp], received.at[tp], local_sem.at[2])
    label_rows = [labels[part].astype(jnp.float32) for part in range(N_TP)]
    for targets in attend(qv, keys, label_rows, store, causal):
        for target in targets:

            @pl.when(tp != target)
            def _():
                head_copy(target).start()

    keep_heads.start()
    keep_heads.wait()
    for target in range(N_TP):

        @pl.when(tp != target)
        def _():
            arrival = pltpu.make_async_remote_copy(
                src_ref=heads.at[target],
                dst_ref=received.at[target],
                send_sem=head_send.at[target],
                recv_sem=head_recv.at[target],
                device_id={"tp": target},
                device_id_type=MESH,
            )
            arrival.wait_send()
            arrival.wait_recv()

    for copy in core_copies:
        copy.wait_recv()
    for copy in pending:
        copy.wait_send()


def run_layer(rows, labels, qkv, shard, causal, collective_id):
    row_total, width = rows.shape
    features = qkv.shape[1]
    weights = qkv.reshape(3 * features, width)
    vmem = pl.BlockSpec(memory_space=pltpu.VMEM)
    hbm = pl.BlockSpec(memory_space=pl.ANY)
    dma = pltpu.SemaphoreType.DMA
    bf16 = jnp.bfloat16
    all_shards = jax.ShapeDtypeStruct((N_Z, N_X, SHARD_PAD, width), bf16)
    return pl.pallas_call(
        functools.partial(layer_kernel, causal),
        out_shape=[
            jax.ShapeDtypeStruct((N_TP, features, row_total), bf16),
            all_shards,
            all_shards,
        ],
        in_specs=[vmem, vmem, vmem, hbm],
        out_specs=[hbm] * 3,
        scratch_shapes=[
            pltpu.VMEM((N_TP, row_total, width), bf16),
            pltpu.VMEM((N_TP, *labels.shape), labels.dtype),
            pltpu.VMEM(weights.shape, bf16),
            pltpu.VMEM((N_TP, 2 * features, row_total), bf16),
            pltpu.VMEM((features // HEAD_DIM, N_TP * row_total, HEAD_DIM), bf16),
            pltpu.VMEM((N_TP, features, row_total), bf16),
            pltpu.VMEM((SHARD_PAD, width), bf16),
            dma((16,)),
            dma((16,)),
            dma((8,)),
            dma((8,)),
            dma((16,)),
            dma((16,)),
            dma((3,)),
            dma((3,)),
            dma((10,)),
            dma((10,)),
            dma((8,)),
            dma((8,)),
            dma((3,)),
        ],
        compiler_params=pltpu.CompilerParams(collective_id=collective_id, has_side_effects=True),
    )(rows, labels, shard, weights)


def merge_kernel(own, weights_hbm, out, slots, weights, results, image, *sems):
    row_send, row_recv, col_send, col_recv, local_sem = sems
    tp = lax.axis_index("tp")
    half = own.shape[0] // 2
    greet([{"tp": wrap(tp + d, N_TP)} for d in range(1, N_TP)])
    neighbours = [{"tp": wrap(tp + 1, N_TP)}, {"tp": wrap(tp - 1, N_TP)}]

    def block_of(way, step):
        return wrap(tp - step, N_TP) if way == 0 else wrap(tp + step, N_TP)

    def row_copy(way, step, part):
        span = pl.ds(part * half, half)
        dst = slots.at[block_of(way, step), span]
        slot = (way * 4 + step) * 2 + part
        return pltpu.make_async_remote_copy(
            src_ref=own.at[span] if step == 0 else dst,
            dst_ref=dst,
            send_sem=row_send.at[slot],
            recv_sem=row_recv.at[slot],
            device_id=neighbours[way],
            device_id_type=MESH,
        )

    pending = []
    ring = {}

    def start(way, step, part):
        ring[way, step, part] = row_copy(way, step, part)
        ring[way, step, part].start()
        pending.append(ring[way, step, part])

    for part in range(2):
        for way in range(2):
            start(way, 0, part)
    fetch = pltpu.make_async_copy(weights_hbm, weights, local_sem.at[0])
    fetch.start()
    fetch.wait()

    def columns(block):
        return times_transpose(block, weights[...]).astype(jnp.bfloat16)

    results[tp] = columns(own[...])
    keep = pltpu.make_async_copy(results.at[tp], image.at[tp], local_sem.at[1])
    keep.start()
    arrivals = []

    def give(way, step):
        block = block_of(way, step)
        results[block] = columns(slots[block])
        copy = pltpu.make_async_remote_copy(
            src_ref=results.at[block],
            dst_ref=image.at[tp],
            send_sem=col_send.at[way * 5 + step],
            recv_sem=col_recv.at[way * 5 + step],
            device_id={"tp": block},
            device_id_type=MESH,
        )
        copy.start()
        pending.append(copy)
        arrivals.append(copy)

    for step in range(1, 4):
        for part in range(2):
            for way in range(2):
                ring[way, step - 1, part].wait_recv()
                if step < 3 or part == way:
                    start(way, step, part)
        for way in range(2):
            give(way, step)
    for way in range(2):
        ring[way, 3, way].wait_recv()
    give(0, 4)
    keep.wait()
    for copy in arrivals:
        copy.wait_recv()
    out[...] = jnp.concatenate(
        [image[part].astype(jnp.float32) for part in range(N_TP)], axis=1
    ).astype(jnp.bfloat16)
    for copy in pending:
        copy.wait_send()


def merge_rows(merged, merge_w, collective_id):
    row_total, depth = merged.shape
    features = merge_w.shape[0]
    hbm = pl.BlockSpec(memory_space=pl.ANY)
    dma = pltpu.SemaphoreType.DMA
    return pl.pallas_call(
        merge_kernel,
        out_shape=jax.ShapeDtypeStruct((row_total, N_TP * features), jnp.bfloat16),
        in_specs=[pl.BlockSpec(memory_space=pltpu.VMEM), hbm],
        out_specs=pl.BlockSpec(memory_space=pltpu.VMEM),
        scratch_shapes=[
            pltpu.VMEM((N_TP, row_total, depth), jnp.bfloat16),
            pltpu.VMEM((features, depth), jnp.bfloat16),
            pltpu.VMEM((N_TP, row_total, features), jnp.bfloat16),
            pltpu.VMEM((N_TP, row_total, features), jnp.bfloat16),
            dma((16,)),
            dma((16,)),
            dma((10,)),
            dma((10,)),
            dma((2,)),
        ],
        compiler_params=pltpu.CompilerParams(collective_id=collective_id, has_side_effects=True),
    )(merged, merge_w)


def attention_layer(rows, labels, qkv, columns, causal, first_id):
    own_heads, shards, other = run_layer(rows, labels, qkv, columns.T, causal, first_id)
    own_heads = own_heads.reshape(rows.shape[1], rows.shape[0])

    def project(part):
        flat = part.reshape(N_Z * N_X * SHARD_PAD, rows.shape[1])
        return jnp.dot(flat, own_heads, preferred_element_type=jnp.float32)

    here, there = project(shards), project(other)
    first = lax.rem(lax.axis_index("grp"), 2) == 0
    both = jnp.stack([jnp.where(first, here, there), jnp.where(first, there, here)])
    both = both.reshape(2, N_Z, N_X, SHARD_PAD, rows.shape[0])[:, :, :, :SHARD]
    projected = both.transpose(4, 2, 1, 0, 3).reshape(rows.shape)
    return (rows.astype(jnp.float32) + projected).astype(jnp.bfloat16)


def per_device(
    patches, pictures, vis_qkv, vis_out, merge_w, text, places, segments, txt_qkv, txt_out
):
    tp_count = lax.axis_size("tp")
    grp_count = lax.axis_size("grp")
    width = patches.shape[1]
    vis_hidden = attention_layer(patches, pictures, vis_qkv, vis_out, False, 0)
    merged = layer_norm(vis_hidden).reshape(patches.shape[0] // 4, 4 * width)
    row_total = places.shape[0]
    image_rows = merge_rows(merged, merge_w, 2)
    tok_count = text.shape[0]
    group_tokens = tok_count * tp_count
    dest_group = places // group_tokens
    dest_local = places % tok_count
    row_ids = jnp.arange(row_total, dtype=jnp.int32)
    earlier = row_ids[:, None] > row_ids[None, :]
    same_dest = dest_group[:, None] == dest_group[None, :]
    slot_rank = jnp.sum((earlier & same_dest).astype(jnp.int32), axis=1)
    slot_index = dest_group * SEND_CAP + slot_rank
    slot_ids = jnp.arange(grp_count * SEND_CAP, dtype=jnp.int32)
    slot_pick = (slot_ids[:, None] == slot_index[None, :]).astype(jnp.bfloat16)
    marks = jnp.broadcast_to((dest_local + 1)[:, None], (row_total, LANES)).astype(jnp.bfloat16)
    send_rows = jnp.dot(
        slot_pick,
        jnp.concatenate([image_rows, marks], axis=1),
        preferred_element_type=jnp.float32,
    ).astype(jnp.bfloat16)
    send_rows = send_rows.reshape(grp_count, SEND_CAP, width + LANES)
    recv = lax.all_to_all(send_rows, "grp", split_axis=0, concat_axis=0, tiled=True)
    recv = recv.reshape(grp_count * SEND_CAP, width + LANES)
    recv_rows = recv[:, :width]
    recv_pos = recv[:, width].astype(jnp.int32) - 1
    position_hit = jnp.arange(tok_count, dtype=jnp.int32)[:, None] == recv_pos[None, :]
    placed = jnp.dot(
        position_hit.astype(jnp.bfloat16), recv_rows, preferred_element_type=jnp.float32
    ).astype(jnp.bfloat16)
    covered = jnp.any(position_hit, axis=1)
    prompt = jnp.where(covered[:, None], placed, text)
    return attention_layer(prompt, segments, txt_qkv, txt_out, True, 4)


def solution(mesh):
    placed = (
        P(("grp", "tp"), None),
        P("grp", "tp"),
        P(None, "tp", None),
        P(None, "grp"),
        P("tp", None),
        P(("grp", "tp"), None),
        P(("grp", "tp")),
        P("grp", "tp"),
        P(None, "tp", None),
        P(None, "grp"),
    )
    return jax.shard_map(
        per_device, mesh=mesh, in_specs=placed, out_specs=P(("grp", "tp"), None), check_vma=False
    )
```

```python
import functools

import jax
import jax.numpy as jnp
from jax import lax
from jax.experimental import pallas as pl
from jax.experimental.pallas import tpu as pltpu
from jax.sharding import PartitionSpec as P

HEAD_DIM = 80
SEND_CAP = 2
N_TP = 8
N_Z = 8
N_X = 4
SHARD = 20
SHARD_PAD = 24
LANES = 128


EPSILON = 1e-05
MASKED = -1e30
MESH = pl.DeviceIdType.MESH


def layer_norm(rows):
    widened = rows.astype(jnp.float32)
    row_mean = jnp.mean(widened, axis=-1, keepdims=True)
    centred = widened - row_mean
    spread = jnp.mean(centred * centred, axis=-1, keepdims=True)
    return (centred * lax.rsqrt(spread + EPSILON)).astype(jnp.bfloat16)


def times_transpose(left, right):
    return lax.dot_general(
        left, right, (((1,), (1,)), ((), ())), preferred_element_type=jnp.float32
    )


def wrap(value, count):
    return lax.rem(value + count, count)


def greet(devices):
    barrier = pltpu.get_barrier_semaphore()
    for device in devices:
        pl.semaphore_signal(barrier, inc=1, device_id=device, device_id_type=MESH)
    pl.semaphore_wait(barrier, len(devices))


Q_BLOCK = 256


def attend(qv, keys, label_rows, store, causal):
    heads_here, row_count = keys.shape[:2]
    factor = HEAD_DIM ** (-0.5) * 1.4426950408889634
    key_labels = jnp.concatenate(
        [jnp.broadcast_to(label, (LANES, LANES)).T for label in label_rows], axis=0
    )
    lanes_per = Q_BLOCK // LANES
    for block in range(row_count // Q_BLOCK):
        first = block * Q_BLOCK
        targets = range(block * lanes_per, (block + 1) * lanes_per)
        end_key = first + Q_BLOCK if causal else row_count
        allowed = jnp.concatenate(
            [key_labels[:end_key] == label_rows[target] for target in targets], axis=1
        )
        if causal:
            key_ids = lax.broadcasted_iota(jnp.int32, (end_key, Q_BLOCK), 0)
            query_ids = lax.broadcasted_iota(jnp.int32, (end_key, Q_BLOCK), 1) + first
            allowed = allowed & (query_ids >= key_ids)
        for head in range(heads_here):
            here = slice(head * HEAD_DIM, (head + 1) * HEAD_DIM)
            after = (heads_here + head) * HEAD_DIM
            queries = jnp.concatenate([qv[target, here, :] for target in targets], axis=1)
            values = jnp.concatenate(
                [qv[part, after : after + HEAD_DIM, :] for part in range(end_key // LANES)],
                axis=1,
            )
            scores = jnp.dot(
                keys[head, :end_key, :], queries, preferred_element_type=jnp.float32
            )
            scores = jnp.where(allowed, scores, MASKED)
            top = jnp.max(scores, axis=0, keepdims=True)
            weights = jnp.exp2((scores - top) * factor)
            total = jnp.sum(weights, axis=0, keepdims=True)
            mixed = jnp.dot(
                values, weights.astype(jnp.bfloat16), preferred_element_type=jnp.float32
            )
            store(targets, here, (mixed / total).astype(jnp.bfloat16))
        yield targets


def layer_kernel(causal, *refs):
    own, own_label, columns, weights_hbm, received, shards, other = refs[:7]
    slots, labels, weights, qv, keys, heads, own_shard = refs[7:14]
    row_send, row_recv, lab_send, lab_recv, z_send, z_recv = refs[14:20]
    x_send, x_recv, core_send, core_recv, head_send, head_recv, local_sem = refs[20:]
    tp = lax.axis_index("tp")
    grp = lax.axis_index("grp")
    core = lax.rem(grp, 2)
    z_here = lax.rem(grp // 2, N_Z)
    x_here = grp // (2 * N_Z)
    half = own.shape[0] // 2
    features = heads.shape[1]

    def at_xz(x, z):
        return {"grp": (x * N_Z + z) * 2 + core}

    partner = {"grp": grp + 1 - 2 * core}
    tp_next = [{"tp": wrap(tp + 1, N_TP)}, {"tp": wrap(tp - 1, N_TP)}]
    z_next = [at_xz(x_here, wrap(z_here + 1, N_Z)), at_xz(x_here, wrap(z_here - 1, N_Z))]
    x_peers = [at_xz(wrap(x_here + d, N_X), z_here) for d in range(1, N_X)]

    fetch = pltpu.make_async_copy(weights_hbm, weights, local_sem.at[0])
    fetch.start()
    own_place = shards.at[z_here, x_here]
    own_shard[...] = jnp.zeros_like(own_shard)
    own_shard[: columns.shape[0], :] = columns[...]
    slots[tp] = layer_norm(own[...])
    labels[tp] = own_label[...]
    greet([{"tp": wrap(tp + d, N_TP)} for d in range(1, N_TP)] + z_next + x_peers + [partner])

    pending = []

    def send(src, dst, send_sem, recv_sem, device):
        copy = pltpu.make_async_remote_copy(
            src_ref=src,
            dst_ref=dst,
            send_sem=send_sem,
            recv_sem=recv_sem,
            device_id=device,
            device_id_type=MESH,
        )
        copy.start()
        pending.append(copy)
        return copy

    def block_of(way, step):
        return wrap(tp - step, N_TP) if way == 0 else wrap(tp + step, N_TP)

    def z_block(way, step):
        return wrap(z_here - step, N_Z) if way == 0 else wrap(z_here + step, N_Z)

    def row_copy(way, step, part):
        place = slots.at[block_of(way, step), pl.ds(part * half, half)]
        slot = (way * 4 + step) * 2 + part
        return send(place, place, row_send.at[slot], row_recv.at[slot], tp_next[way])

    def label_copy(way, step):
        place = labels.at[block_of(way, step)]
        slot = way * 4 + step
        return send(place, place, lab_send.at[slot], lab_recv.at[slot], tp_next[way])

    def shard_copy(way, step, part):
        place = shards.at[z_block(way, step), pl.ds(part * 2, 2)]
        slot = (way * 4 + step) * 2 + part
        return send(place, place, z_send.at[slot], z_recv.at[slot], z_next[way])

    core_copies = []

    def core_copy(way, step):
        block = z_block(way, step)
        slot = way * 5 + step
        core_copies.append(
            send(shards.at[block], other.at[block], core_send.at[slot], core_recv.at[slot], partner)
        )

    def project(block):
        found = lax.dot_general(
            weights[...],
            slots[block],
            (((1,), (1,)), ((), ())),
            preferred_element_type=jnp.float32,
        )
        qv[block, :features, :] = found[:features].astype(jnp.bfloat16)
        qv[block, features:, :] = found[2 * features :].astype(jnp.bfloat16)
        place = pl.ds(pl.multiple_of(block * LANES, LANES), LANES)
        for head in range(features // HEAD_DIM):
            begin = features + head * HEAD_DIM
            keys[head, place, :] = found[begin : begin + HEAD_DIM].T.astype(jnp.bfloat16)

    row_ring, label_ring, shard_ring = {}, {}, {}
    for part in range(2):
        for way in range(2):
            row_ring[way, 0, part] = row_copy(way, 0, part)
    for way in range(2):
        label_ring[way, 0] = label_copy(way, 0)
    x_copies = [
        send(own_shard, own_place, x_send.at[d], x_recv.at[d], x_peers[d]) for d in range(N_X - 1)
    ]
    keep_shard = pltpu.make_async_copy(own_shard, own_place, local_sem.at[1])
    keep_shard.start()
    fetch.wait()
    project(tp)

    def shard_step(step):
        if step == 0:
            keep_shard.wait()
            for copy in x_copies:
                copy.wait_recv()
        for part in range(2):
            for way in range(2):
                if step and (step < 4 or part == way):
                    shard_ring[way, step - 1, part].wait_recv()
                if step < 3 or (step == 3 and part == way):
                    shard_ring[way, step, part] = shard_copy(way, step, part)
        for way in range(2 if step in (1, 2, 3) else 1):
            core_copy(way, step)

    shard_step(0)
    for step in range(1, 4):
        for part in range(2):
            for way in range(2):
                row_ring[way, step - 1, part].wait_recv()
                if step < 3 or part == way:
                    row_ring[way, step, part] = row_copy(way, step, part)
        for way in range(2):
            label_ring[way, step - 1].wait_recv()
            if step < 3 or way == 0:
                label_ring[way, step] = label_copy(way, step)
        for way in range(2):
            project(block_of(way, step))
        shard_step(step)
    for way in range(2):
        row_ring[way, 3, way].wait_recv()
    label_ring[0, 3].wait_recv()
    project(block_of(0, 4))
    def store(targets, here, mixed):
        for index, target in enumerate(targets):
            heads[target, here, :] = mixed[:, index * LANES : (index + 1) * LANES]

    def head_copy(target):
        return pltpu.make_async_remote_copy(
            src_ref=heads.at[target],
            dst_ref=received.at[tp],
            send_sem=head_send.at[target],
            recv_sem=head_recv.at[tp],
            device_id={"tp": target},
            device_id_type=MESH,
        )

    keep_heads = pltpu.make_async_copy(heads.at[tp], received.at[tp], local_sem.at[2])
    label_rows = [labels[part].astype(jnp.float32) for part in range(N_TP)]
    for done, targets in enumerate(attend(qv, keys, label_rows, store, causal)):
        if done == 0:
            shard_step(4)
        for target in targets:

            @pl.when(tp != target)
            def _():
                head_copy(target).start()

    keep_heads.start()
    keep_heads.wait()
    for target in range(N_TP):

        @pl.when(tp != target)
        def _():
            arrival = pltpu.make_async_remote_copy(
                src_ref=heads.at[target],
                dst_ref=received.at[target],
                send_sem=head_send.at[target],
                recv_sem=head_recv.at[target],
                device_id={"tp": target},
                device_id_type=MESH,
            )
            arrival.wait_send()
            arrival.wait_recv()

    for copy in core_copies:
        copy.wait_recv()
    for copy in pending:
        copy.wait_send()


def run_layer(rows, labels, qkv, shard, causal, collective_id):
    row_total, width = rows.shape
    features = qkv.shape[1]
    weights = qkv.reshape(3 * features, width)
    vmem = pl.BlockSpec(memory_space=pltpu.VMEM)
    hbm = pl.BlockSpec(memory_space=pl.ANY)
    dma = pltpu.SemaphoreType.DMA
    bf16 = jnp.bfloat16
    all_shards = jax.ShapeDtypeStruct((N_Z, N_X, SHARD_PAD, width), bf16)
    return pl.pallas_call(
        functools.partial(layer_kernel, causal),
        out_shape=[
            jax.ShapeDtypeStruct((N_TP, features, row_total), bf16),
            all_shards,
            all_shards,
        ],
        in_specs=[vmem, vmem, vmem, hbm],
        out_specs=[hbm] * 3,
        scratch_shapes=[
            pltpu.VMEM((N_TP, row_total, width), bf16),
            pltpu.VMEM((N_TP, *labels.shape), labels.dtype),
            pltpu.VMEM(weights.shape, bf16),
            pltpu.VMEM((N_TP, 2 * features, row_total), bf16),
            pltpu.VMEM((features // HEAD_DIM, N_TP * row_total, HEAD_DIM), bf16),
            pltpu.VMEM((N_TP, features, row_total), bf16),
            pltpu.VMEM((SHARD_PAD, width), bf16),
            dma((16,)),
            dma((16,)),
            dma((8,)),
            dma((8,)),
            dma((16,)),
            dma((16,)),
            dma((3,)),
            dma((3,)),
            dma((10,)),
            dma((10,)),
            dma((8,)),
            dma((8,)),
            dma((3,)),
        ],
        compiler_params=pltpu.CompilerParams(collective_id=collective_id, has_side_effects=True),
    )(rows, labels, shard, weights)


def merge_kernel(own, weights_hbm, out, slots, weights, results, image, *sems):
    row_send, row_recv, col_send, col_recv, local_sem = sems
    tp = lax.axis_index("tp")
    half = own.shape[0] // 2
    greet([{"tp": wrap(tp + d, N_TP)} for d in range(1, N_TP)])
    neighbours = [{"tp": wrap(tp + 1, N_TP)}, {"tp": wrap(tp - 1, N_TP)}]

    def block_of(way, step):
        return wrap(tp - step, N_TP) if way == 0 else wrap(tp + step, N_TP)

    def row_copy(way, step, part):
        span = pl.ds(part * half, half)
        dst = slots.at[block_of(way, step), span]
        slot = (way * 4 + step) * 2 + part
        return pltpu.make_async_remote_copy(
            src_ref=own.at[span] if step == 0 else dst,
            dst_ref=dst,
            send_sem=row_send.at[slot],
            recv_sem=row_recv.at[slot],
            device_id=neighbours[way],
            device_id_type=MESH,
        )

    pending = []
    ring = {}

    def start(way, step, part):
        ring[way, step, part] = row_copy(way, step, part)
        ring[way, step, part].start()
        pending.append(ring[way, step, part])

    for part in range(2):
        for way in range(2):
            start(way, 0, part)
    fetch = pltpu.make_async_copy(weights_hbm, weights, local_sem.at[0])
    fetch.start()
    fetch.wait()

    def columns(block):
        return times_transpose(block, weights[...]).astype(jnp.bfloat16)

    results[tp] = columns(own[...])
    keep = pltpu.make_async_copy(results.at[tp], image.at[tp], local_sem.at[1])
    keep.start()
    arrivals = []

    def give(way, step):
        block = block_of(way, step)
        results[block] = columns(slots[block])
        copy = pltpu.make_async_remote_copy(
            src_ref=results.at[block],
            dst_ref=image.at[tp],
            send_sem=col_send.at[way * 5 + step],
            recv_sem=col_recv.at[way * 5 + step],
            device_id={"tp": block},
            device_id_type=MESH,
        )
        copy.start()
        pending.append(copy)
        arrivals.append(copy)

    for step in range(1, 4):
        for part in range(2):
            for way in range(2):
                ring[way, step - 1, part].wait_recv()
                if step < 3 or part == way:
                    start(way, step, part)
        for way in range(2):
            give(way, step)
    for way in range(2):
        ring[way, 3, way].wait_recv()
    give(0, 4)
    keep.wait()
    for copy in arrivals:
        copy.wait_recv()
    out[...] = jnp.concatenate(
        [image[part].astype(jnp.float32) for part in range(N_TP)], axis=1
    ).astype(jnp.bfloat16)
    for copy in pending:
        copy.wait_send()


def merge_rows(merged, merge_w, collective_id):
    row_total, depth = merged.shape
    features = merge_w.shape[0]
    hbm = pl.BlockSpec(memory_space=pl.ANY)
    dma = pltpu.SemaphoreType.DMA
    return pl.pallas_call(
        merge_kernel,
        out_shape=jax.ShapeDtypeStruct((row_total, N_TP * features), jnp.bfloat16),
        in_specs=[pl.BlockSpec(memory_space=pltpu.VMEM), hbm],
        out_specs=pl.BlockSpec(memory_space=pltpu.VMEM),
        scratch_shapes=[
            pltpu.VMEM((N_TP, row_total, depth), jnp.bfloat16),
            pltpu.VMEM((features, depth), jnp.bfloat16),
            pltpu.VMEM((N_TP, row_total, features), jnp.bfloat16),
            pltpu.VMEM((N_TP, row_total, features), jnp.bfloat16),
            dma((16,)),
            dma((16,)),
            dma((10,)),
            dma((10,)),
            dma((2,)),
        ],
        compiler_params=pltpu.CompilerParams(collective_id=collective_id, has_side_effects=True),
    )(merged, merge_w)


def attention_layer(rows, labels, qkv, columns, causal, first_id):
    own_heads, shards, other = run_layer(rows, labels, qkv, columns.T, causal, first_id)
    own_heads = own_heads.reshape(rows.shape[1], rows.shape[0])

    def project(part):
        flat = part.reshape(N_Z * N_X * SHARD_PAD, rows.shape[1])
        return jnp.dot(flat, own_heads, preferred_element_type=jnp.float32)

    here, there = project(shards), project(other)
    first = lax.rem(lax.axis_index("grp"), 2) == 0
    both = jnp.stack([jnp.where(first, here, there), jnp.where(first, there, here)])
    both = both.reshape(2, N_Z, N_X, SHARD_PAD, rows.shape[0])[:, :, :, :SHARD]
    projected = both.transpose(4, 2, 1, 0, 3).reshape(rows.shape)
    return (rows.astype(jnp.float32) + projected).astype(jnp.bfloat16)


def per_device(
    patches, pictures, vis_qkv, vis_out, merge_w, text, places, segments, txt_qkv, txt_out
):
    tp_count = lax.axis_size("tp")
    grp_count = lax.axis_size("grp")
    width = patches.shape[1]
    vis_hidden = attention_layer(patches, pictures, vis_qkv, vis_out, False, 0)
    merged = layer_norm(vis_hidden).reshape(patches.shape[0] // 4, 4 * width)
    row_total = places.shape[0]
    image_rows = merge_rows(merged, merge_w, 2)
    tok_count = text.shape[0]
    group_tokens = tok_count * tp_count
    dest_group = places // group_tokens
    dest_local = places % tok_count
    row_ids = jnp.arange(row_total, dtype=jnp.int32)
    earlier = row_ids[:, None] > row_ids[None, :]
    same_dest = dest_group[:, None] == dest_group[None, :]
    slot_rank = jnp.sum((earlier & same_dest).astype(jnp.int32), axis=1)
    slot_index = dest_group * SEND_CAP + slot_rank
    slot_ids = jnp.arange(grp_count * SEND_CAP, dtype=jnp.int32)
    slot_pick = (slot_ids[:, None] == slot_index[None, :]).astype(jnp.bfloat16)
    marks = jnp.broadcast_to((dest_local + 1)[:, None], (row_total, LANES)).astype(jnp.bfloat16)
    send_rows = jnp.dot(
        slot_pick,
        jnp.concatenate([image_rows, marks], axis=1),
        preferred_element_type=jnp.float32,
    ).astype(jnp.bfloat16)
    send_rows = send_rows.reshape(grp_count, SEND_CAP, width + LANES)
    recv = lax.all_to_all(send_rows, "grp", split_axis=0, concat_axis=0, tiled=True)
    recv = recv.reshape(grp_count * SEND_CAP, width + LANES)
    recv_rows = recv[:, :width]
    recv_pos = recv[:, width].astype(jnp.int32) - 1
    position_hit = jnp.arange(tok_count, dtype=jnp.int32)[:, None] == recv_pos[None, :]
    placed = jnp.dot(
        position_hit.astype(jnp.bfloat16), recv_rows, preferred_element_type=jnp.float32
    ).astype(jnp.bfloat16)
    covered = jnp.any(position_hit, axis=1)
    prompt = jnp.where(covered[:, None], placed, text)
    return attention_layer(prompt, segments, txt_qkv, txt_out, True, 4)


def solution(mesh):
    placed = (
        P(("grp", "tp"), None),
        P("grp", "tp"),
        P(None, "tp", None),
        P(None, "grp"),
        P("tp", None),
        P(("grp", "tp"), None),
        P(("grp", "tp")),
        P("grp", "tp"),
        P(None, "tp", None),
        P(None, "grp"),
    )
    return jax.shard_map(
        per_device, mesh=mesh, in_specs=placed, out_specs=P(("grp", "tp"), None), check_vma=False
    )
```
